32 devices in a mesh: row: 8 (over z, x), col: 2 (over y), rep: 2 (over core).
Axes of the slice: x: 2, y: 2, z: 4, core: 2. Of those that a mesh axis runs over, the one named last changes fastest.
Arguments:
- rhs_low: float32 [2, 3, 8, 256, 128], P('rep', None, 'row', 'col'), may hold values from -6 to 6
- rhs_top: float32 [8, 256, 128], P('row', 'col'), may hold values from -6 to 6
- inv_low: float32 [2, 3, 8, 256, 256], P('rep', None, 'row', 'col'), as said below
- inv_top: float32 [8, 256, 256], P('row', 'col'), as said below
- blocks: float32 [2, 8, 2, 3, 4, 256, 256], P('rep', 'row', 'col'), may hold values from -0.1875 to 0.1875
- slot_map: int32 [2, 8, 2, 3, 4, 2], P('rep', 'row', 'col'), may hold values from 0 to 3, as said below
Outputs:
- sol_low: float32 [2, 3, 8, 256, 128], P('rep', None, 'row', 'col')
- sol_top: float32 [8, 256, 128], P('row', 'col')
The draws below stay inside these ranges and needn't reach their ends.
Inputs may be any that keep to these rules, and one draw needn't show every extreme that they name: slot_map[s, p, q, l, k] = (t, c): t = 0 marks an empty slot (then c = 0); else 3 >= t > l and c < 4. The live pairs (t, c) of one device and one l are distinct, live slots come before empty ones, every device has at least one live slot for each l, and for each l some device has all 4 slots live. `inv_low`: each block is a dense matrix with a positive diagonal of about one and full off-diagonal entries. `inv_top`: each block is a dense matrix with a positive diagonal of about one and full off-diagonal entries.
All inputs are finite; a program needn't handle non-finite values.
Results may differ from the reference program's by a relative error of at most 0.0003.
Values sent between devices are 32-bit elements; how exact they have to be, the bound alone decides.
A program may use at most 64 MiB of HBM per device.

```python
import math
import jax
import jax.numpy as jnp
from jax import lax

B = 256
R = 128
LOWER = 3
KL = 4
NODES = 8
GRID_COLS = 2
SUBTREES = 2


def inverse_blocks(key, leading):
    key_diag, key_rest = jax.random.split(jax.random.fold_in(key, 11))
    diagonal = jax.random.uniform(key_diag, leading + (B,), jnp.float32, 0.5, 2.0)
    spread = jax.random.normal(key_rest, leading + (B, B), jnp.float32) * (0.6 / math.sqrt(B))
    return spread + diagonal[..., None] * jnp.eye(B, dtype=jnp.float32)


def draw_inv_low(key, part):
    return inverse_blocks(key, (SUBTREES, LOWER, NODES))


def draw_inv_top(key, part):
    return inverse_blocks(key, (NODES,))


def draw_slot_map(key, part):
    col_share = NODES // GRID_COLS
    devices = SUBTREES * NODES * GRID_COLS
    stacks = []
    for height in range(LOWER):
        candidates = (LOWER - height) * col_share
        key_score, key_count, key_full = jax.random.split(jax.random.fold_in(key, 100 + height), 3)
        scores = jax.random.randint(key_score, (devices, candidates), 0, 2 ** 20) * candidates + jnp.arange(candidates, dtype=jnp.int32)
        ranking = jnp.argsort(scores, axis=1)[:, :KL].astype(jnp.int32)
        row_levels = height + 1 + ranking // col_share
        column_ids = ranking % col_share
        counts = jax.random.randint(key_count, (devices,), 1, KL + 1)
        fullest = jax.random.randint(key_full, (), 0, devices)
        counts = jnp.where(jnp.arange(devices) == fullest, KL, counts)
        filled = jnp.arange(KL)[None, :] < counts[:, None]
        stacks.append(jnp.stack([jnp.where(filled, row_levels, 0), jnp.where(filled, column_ids, 0)], axis=-1))
    stacked = jnp.stack(stacks, axis=1)
    return stacked.reshape((SUBTREES, NODES, GRID_COLS, LOWER, KL, 2)).astype(jnp.int32)


def steps_of(rng, shape, cuts, smallest, largest):
    def one(position, blocks):
        draws = jax.random.uniform(jax.random.fold_in(jax.random.fold_in(rng, 6), position), (blocks,), jnp.float32, smallest / len(cuts), largest / len(cuts))
        return jnp.repeat(jnp.exp(draws), shape[position] // blocks).reshape((-1,) + (1,) * (len(shape) - position - 1))

    level = one(*cuts[0])
    for cut in cuts[1:]:
        level = level * one(*cut)
    return level


def noise(key, dims, width, bound, shards=(), kind=jnp.bfloat16):
    factor_of = steps_of(key, dims, shards, -0.22, 0.18) if shards else 1.0
    entries = jax.random.normal(key, dims, jnp.float32) * width * factor_of
    return jnp.minimum(jnp.maximum(entries, -bound), bound).astype(kind)


def setup_inputs(seed: int = 0) -> dict:
    arg_keys = jax.random.split(jax.random.key(seed), 7)
    rhs_low = noise(arg_keys[0], (SUBTREES, LOWER, NODES, B, R), 1.0, 6.0, ((0, 2), (2, 8), (3, 2)), jnp.float32)
    rhs_top = noise(arg_keys[1], (NODES, B, R), 1.0, 6.0, ((0, 8), (1, 2)), jnp.float32)
    inv_low = draw_inv_low(jax.random.fold_in(arg_keys[6], 71), 0)
    inv_top = draw_inv_top(jax.random.fold_in(arg_keys[6], 71), 0)
    blocks = noise(arg_keys[4], (SUBTREES, NODES, GRID_COLS, LOWER, KL, B, B), (B * GRID_COLS * 2) ** -0.5, 0.1875, ((0, 2), (1, 8), (2, 2)), jnp.float32)
    slot_map = draw_slot_map(jax.random.fold_in(arg_keys[6], 71), 0)
    return {"rhs_low": rhs_low, "rhs_top": rhs_top, "inv_low": inv_low, "inv_top": inv_top, "blocks": blocks, "slot_map": slot_map}


def level_terms(block_set, slot_rows, level_sol):
    col_count = block_set.shape[0]
    column_ids = slot_rows[..., 1] * col_count + jnp.arange(col_count, dtype=jnp.int32)[:, None]
    selected = jnp.take(level_sol, column_ids.astype(jnp.int32), axis=0)
    product = jnp.einsum('qkab,qkbr->qkar', block_set, selected, precision=lax.Precision.HIGHEST)
    selector = (slot_rows[..., 0][..., None] == jnp.arange(LOWER + 1, dtype=jnp.int32)).astype(jnp.float32)
    return jnp.einsum('qkt,qkar->tar', selector, product, precision=lax.Precision.HIGHEST)


def reference(rhs_low, rhs_top, inv_low, inv_top, blocks, slot_map):
    highest = lax.Precision.HIGHEST
    rep_count = rhs_low.shape[0]
    node_count = rhs_low.shape[2]
    updates = jnp.zeros((rep_count, LOWER + 1, node_count, B, R), jnp.float32)
    solutions = []
    for height in range(LOWER):
        residue = rhs_low[:, height] - updates[:, height]
        solution = jnp.einsum('spab,spbr->spar', inv_low[:, height], residue, precision=highest)
        solutions.append(solution)
        block_set = blocks[:, :, :, height].reshape((rep_count * node_count,) + blocks.shape[2:3] + blocks.shape[4:])
        slot_rows = slot_map[:, :, :, height].reshape((rep_count * node_count,) + slot_map.shape[2:3] + slot_map.shape[4:])

        def one_row(member):
            return level_terms(block_set[member], slot_rows[member], solution[member // node_count])

        terms = lax.map(one_row, jnp.arange(rep_count * node_count, dtype=jnp.int32))
        terms = terms.reshape((rep_count, node_count, LOWER + 1, B, R))
        updates = updates + jnp.transpose(terms, (0, 2, 1, 3, 4))
    residue = rhs_top - jnp.sum(updates[:, LOWER], axis=0)
    top_rows = jnp.einsum('pab,pbr->par', inv_top, residue, precision=highest)
    return jnp.stack(solutions, axis=1), top_rows
```

```python
import functools
import jax
import jax.numpy as jnp
from jax import lax
from jax.experimental import pallas as pl
from jax.experimental.pallas import tpu as pltpu
from jax.sharding import PartitionSpec as P

MESH = pl.DeviceIdType.MESH
STREAMS = 4
GROUPS = 2
CROSSED = 0


def split(value):
    high = value.astype(jnp.bfloat16)
    low = (value - high.astype(jnp.float32)).astype(jnp.bfloat16)
    return high, low


def dot3(value, right_high, right_low):
    high, low = split(value)
    count = value.shape[0]
    turned = (((1,), (1,)), ((), ()))
    both = jnp.concatenate([high, low], axis=0)
    wide = lax.dot_general(both, right_high, turned, preferred_element_type=jnp.float32)
    rest = lax.dot_general(high, right_low, turned, preferred_element_type=jnp.float32)
    return wide[:count] + (wide[count:] + rest)


def kernel(
    rows, cols, reps, levels, slots, streams, groups,
    rhs_low, rhs_top, inv_low_hbm, inv_top_hbm, blocks_hbm, table_hbm, out_low, out_top,
    table, blocks, inverse, rhs, turned0, right0, partial, give, taken, taken_top, solved, handed, inv_high, inv_rest,
    tile_high, tile_rest,
    table_sem, load_sem, inv_sem, rhs_sem, right_send, right_recv, inv_send, inv_recv, give_send, give_recv,
    top_send, top_recv, col_send, col_recv, hand_send, hand_recv, *columns,
):
    row = lax.axis_index("row")
    q = lax.axis_index("col")
    rep = lax.axis_index("rep")
    share = rows // cols
    group = share // groups
    a = row // cols
    b = row % cols
    home = a // group
    place = a % group
    part = rhs_top.shape[0]
    depth = partial.shape[2]

    def turn(value, by, size):
        return lax.rem(value + by, size)

    def node_row(which, position, line):
        return (which * group + position) * cols + line

    loads = [
        pltpu.make_async_copy(blocks_hbm.at[l], blocks.at[l], load_sem.at[l]) for l in range(levels)
    ]
    inv_loads = [
        pltpu.make_async_copy(inv_low_hbm.at[t] if t < levels else inv_top_hbm, inverse.at[t, q], inv_sem.at[t])
        for t in range(levels + 1)
    ]
    rhs_loads = [
        pltpu.make_async_copy(rhs_low.at[t] if t < levels else rhs_top, rhs.at[t], rhs_sem.at[min(t, 1)])
        for t in range(levels + 1)
    ]
    table_load = pltpu.make_async_copy(table_hbm, table, table_sem)
    for load in [rhs_loads[0], inv_loads[0], inv_loads[1], loads[0]] + rhs_loads[1:] + inv_loads[2:] + loads[1:]:
        load.start()
    table_load.start()

    barrier = pltpu.get_barrier_semaphore()
    peers = set()
    for da in range(group):
        for dx in range(cols):
            for dy in range(cols):
                peers.add((0, da, dx, dy, 0))
    for e in range(groups):
        for dy in range(cols):
            peers.add((e, 0, 0, dy, 0))
    for dy in range(cols):
        for dc in range(reps):
            peers.add((0, 0, 0, dy, dc))
    peers.discard((0, 0, 0, 0, 0))
    for e, da, dx, dy, dc in sorted(peers):
        pl.semaphore_signal(
            barrier, inc=1, device_id_type=MESH,
            device_id={
                "row": node_row(turn(home, e, groups), turn(place, da, group), turn(b, dx, cols)),
                "col": turn(q, dy, cols), "rep": turn(rep, dc, reps),
            },
        )

    def send(src, dst, send_sem, recv_sem, device):
        return pltpu.make_async_remote_copy(
            src_ref=src, dst_ref=dst, send_sem=send_sem, recv_sem=recv_sem,
            device_id=device, device_id_type=MESH,
        )

    def finish(ref, sem):
        pltpu.make_async_copy(ref, ref, sem).wait()

    with jax.named_scope("turn_rhs"):
        finish(rhs.at[0], rhs_sem.at[0])
        first = rhs[0].T
        for s in range(streams):
            turned0[s] = first[s * depth:(s + 1) * depth]
    with jax.named_scope("barrier"):
        pl.semaphore_wait(barrier, len(peers))

    for s in range(streams):
        for d in range(1, cols):
            send(
                turned0.at[s], right0.at[s, cols - d], right_send, right_recv.at[s], {"col": turn(q, d, cols)}
            ).start()

    def give_inverse(t):
        finish(inverse.at[t, q], inv_sem.at[t])
        for d in range(1, cols):
            send(
                inverse.at[t, q], inverse.at[t, q], inv_send, inv_recv.at[t - 1, cols - d], {"col": turn(q, d, cols)}
            ).start()

    def take_inverse(t):
        for d in range(1, cols):
            finish(inverse.at[t, turn(q, d, cols)], inv_recv.at[t - 1, d])
        for h in range(cols):
            high, low = split(inverse[t, h])
            inv_high[t, h * part:(h + 1) * part] = high
            inv_rest[t, h * part:(h + 1) * part] = low

    def take_rhs(t):
        flipped = rhs[t].T
        if t == levels:
            flipped = jnp.where(rep == 0, flipped, 0.0)
        spaced = jnp.concatenate([jnp.where(q == j, flipped, 0.0) for j in range(cols)], axis=1)
        for s in range(streams):
            partial[t, s] = spaced[s * depth:(s + 1) * depth]

    def split_blocks(l):
        finish(blocks.at[l], load_sem.at[l])
        for k in range(slots):
            high, low = split(blocks[l, k])
            tile_high[k] = high
            tile_rest[k] = low

    def crossed(t, s):
        return t > 0 and s < CROSSED

    def offers(t, s):
        for e in reversed(range(groups)):
            for d in reversed(range(cols)):
                if (t == 0 and d) or not (e or d or crossed(t, s)):
                    continue
                h, back = turn(q, d, cols), (groups - e) % groups
                if crossed(t, s):
                    line, col, slot = h, b, lax.rem(q - b + cols, cols)
                else:
                    line, col, slot = b, h, (cols - d) % cols
                copy = send(
                    give.at[t, s, h], taken.at[t, s, back, slot], give_send.at[e, d], give_recv.at[t, s, back],
                    {"row": node_row(turn(home, e, groups), place, line), "col": col},
                )
                if e or d:
                    copy.start()
                else:
                    pl.when(q != b)(copy.start)

                    @pl.when(q == b)
                    def _():
                        pltpu.make_async_copy(give.at[t, s, q], taken.at[t, s, 0, 0], give_recv.at[t, s, 0]).start()

    def contribute(t, s):
        product = dot3(partial[t, s], inv_high[t], inv_rest[t])
        for h in range(cols):
            give[t, s, h] = product[:, h * part:(h + 1) * part]

    def gather(t, s, e):
        if t == 0:
            low, high = 0, 1 if e else 0
        else:
            low, high = 0 if e or crossed(t, s) else 1, cols
        total = None if e or crossed(t, s) else give[t, s, q]
        if high > low:
            with jax.named_scope("gather%d%d%d" % (t, s, e)):
                finish(taken.at[t, s, e, low:high], give_recv.at[t, s, e])
        for d in range(low, high):
            total = taken[t, s, e, d] if total is None else total + taken[t, s, e, d]
        return total

    def spread(l, s, e):
        which = turn(home, e, groups)
        line, col, piece = (q, q, b) if crossed(l, s) else (b, b, q)
        for da in reversed(range(group)):
            for dx in reversed(range(cols)):
                src = solved.at[l * streams + s, e]
                dst = columns[l * streams + s].at[which * group + place, piece]
                device = {"row": node_row(home, turn(place, da, group), turn(b, dx, cols)), "col": col}
                copy = functools.partial(send, src, dst, col_send.at[da, dx], col_recv.at[l, s], device)
                local = functools.partial(pltpu.make_async_copy, src, dst, col_recv.at[l, s])
                if da or dx:
                    copy().start()
                elif crossed(l, s):
                    local().start()
                else:
                    pl.when(q != b)(lambda: copy().start())
                    pl.when(q == b)(lambda: local().start())

    def hand_over(l, s):
        src = solved.at[l * streams + s, 0]
        copy = send(
            src, handed.at[l, s], hand_send, hand_recv.at[l], {"row": node_row(home, place, q), "col": b}
        )
        pl.when(q != b)(copy.start)

        @pl.when(q == b)
        def _():
            pltpu.make_async_copy(src, handed.at[l, s], hand_recv.at[l]).start()

    finish(inverse.at[0, q], inv_sem.at[0])
    high0, low0 = split(inverse[0, q])
    give_inverse(1)
    for s in range(streams):
        with jax.named_scope("rhs_wait%d" % s):
            finish(right0.at[s, 1:cols], right_recv.at[s])
        right0[s, 0] = turned0[s]
        residue = jnp.concatenate([right0[s, turn(cols - q, j, cols)] for j in range(cols)], axis=1)
        give[0, s, q] = dot3(residue, high0, low0)
        offers(0, s)
    table_load.wait()
    split_blocks(0)

    for l in range(levels):
        pieces = []
        for s in range(streams):
            for e in range(groups):
                total = gather(l, s, e)
                if e == 0 and not crossed(l, s):
                    pieces.append(total)
                solved[l * streams + s, e] = total
                spread(l, s, e)
        for s in range(streams):
            if crossed(l, s):
                hand_over(l, s)
        if l == 0:
            with jax.named_scope("take_rhs"):
                finish(rhs.at[1:], rhs_sem.at[1])
                for t in range(1, levels + 1):
                    take_rhs(t)
        if l and CROSSED:
            finish(handed.at[l, :CROSSED], hand_recv.at[l])
            pieces = [handed[l, s] for s in range(CROSSED)] + pieces
        out_low[l] = jnp.concatenate(pieces, axis=0).T
        with jax.named_scope("inverse%d" % l):
            take_inverse(l + 1)
        if l + 2 <= levels:
            give_inverse(l + 2)
        later = []

        def add(t, s, products):
            total = partial[t, s]
            for k in range(slots):
                total = total - jnp.where(table[l, 0, k] == t, products[k], 0.0)
            partial[t, s] = total

        for s in range(streams):
            with jax.named_scope("arrive%d%d" % (l, s)):
                finish(columns[l * streams + s], col_recv.at[l, s])
            with jax.named_scope("multiply%d%d" % (l, s)):
                products = []
                for k in range(slots):
                    found = columns[l * streams + s][table[l, 1, k]]
                    picked = jnp.concatenate([found[j] for j in range(cols)], axis=1)
                    products.append(dot3(picked, tile_high[k], tile_rest[k]))
                later.append((s, products))
                add(l + 1, s, products)
                contribute(l + 1, s)
            if l + 1 < levels:
                offers(l + 1, s)
            else:
                for d in reversed(range(cols)):
                    for r in reversed(range(reps)):
                        if d or r:
                            slot = (cols - d) % cols * reps + (reps - r) % reps - 1
                            send(
                                give.at[levels, s, turn(q, d, cols)], taken_top.at[s, slot], top_send,
                                top_recv.at[s], {"col": turn(q, d, cols), "rep": turn(rep, r, reps)},
                            ).start()
        for s, products in later:
            for t in range(l + 2, levels + 1):
                add(t, s, products)
        if l + 1 < levels:
            split_blocks(l + 1)

    pieces = []
    for s in range(streams):
        with jax.named_scope("top%d" % s):
            finish(taken_top.at[s], top_recv.at[s])
        total = give[levels, s, q]
        for slot in range(cols * reps - 1):
            total = total + taken_top[s, slot]
        pieces.append(total)
    with jax.named_scope("finish"):
        out_top[...] = jnp.concatenate(pieces, axis=0).T

        finish(right0.at[:, 1:cols], right_send)
        finish(inverse.at[1:, 1:cols], inv_send)
        finish(taken_top, top_send)
        for e in range(groups):
            for d in range(cols):
                if e or d:
                    finish(give.at[0 if d == 0 else 1:levels, :, 0], give_send.at[e, d])
        for da in range(group):
            for dx in range(cols):
                if da or dx:
                    finish(solved, col_send.at[da, dx])

        @pl.when(q != b)
        def _():
            plain = levels * streams - (levels - 1) * CROSSED
            finish(solved.at[:plain], col_send.at[0, 0])
            if CROSSED:
                finish(give.at[1:levels, :CROSSED, 0], give_send.at[0, 0])
                finish(handed.at[1:levels, :CROSSED], hand_send)


def per_device(rows, cols, reps, rhs_low, rhs_top, inv_low, inv_top, blocks, slot_map):
    rhs_low, rhs_top = rhs_low[0, :, 0], rhs_top[0]
    inv_low, inv_top = inv_low[0, :, 0], inv_top[0]
    blocks, table = blocks[0, 0, 0], jnp.swapaxes(slot_map[0, 0, 0], 1, 2)
    levels, slots, size = blocks.shape[:3]
    rhs_low, rhs_top, inv_low, inv_top, blocks, table = [
        pltpu.with_memory_space_constraint(x, pltpu.HBM) for x in (rhs_low, rhs_top, inv_low, inv_top, blocks, table)
    ]
    part, width = rhs_top.shape
    share = rows // cols
    streams, groups = STREAMS, GROUPS
    group = share // groups
    depth = width // streams
    vmem = pl.BlockSpec(memory_space=pltpu.VMEM)
    hbm = pl.BlockSpec(memory_space=pltpu.HBM)
    dma = pltpu.SemaphoreType.DMA
    f32, bf16 = jnp.float32, jnp.bfloat16
    sol_low, sol_top = pl.pallas_call(
        functools.partial(kernel, rows, cols, reps, levels, slots, streams, groups),
        out_shape=(
            jax.ShapeDtypeStruct((levels, part, width), f32),
            jax.ShapeDtypeStruct((part, width), f32),
        ),
        in_specs=[hbm, hbm, hbm, hbm, hbm, hbm],
        out_specs=(vmem, vmem),
        scratch_shapes=[
            pltpu.SMEM(table.shape, jnp.int32),
            pltpu.VMEM((levels, slots, size, size), f32),
            pltpu.VMEM((levels + 1, cols, part, size), f32),
            pltpu.VMEM((levels + 1, part, width), f32),
            pltpu.VMEM((streams, depth, part), f32),
            pltpu.VMEM((streams, cols, depth, part), f32),
            pltpu.VMEM((levels + 1, streams, depth, size), f32),
            pltpu.VMEM((levels + 1, streams, cols, depth, part), f32),
            pltpu.VMEM((levels, streams, groups, cols, depth, part), f32),
            pltpu.VMEM((streams, cols * reps - 1, depth, part), f32),
            pltpu.VMEM((levels * streams, groups, depth, part), f32),
            pltpu.VMEM((levels, streams, depth, part), f32),
            pltpu.VMEM((levels + 1, size, size), bf16),
            pltpu.VMEM((levels + 1, size, size), bf16),
            pltpu.VMEM((slots, size, size), bf16),
            pltpu.VMEM((slots, size, size), bf16),
            dma(()),
            dma((levels,)),
            dma((levels + 1,)),
            dma((2,)),
            dma(()),
            dma((streams,)),
            dma(()),
            dma((levels, cols)),
            dma((groups, cols)),
            dma((levels, streams, groups)),
            dma(()),
            dma((streams,)),
            dma((group, cols)),
            dma((levels, streams)),
            dma(()),
            dma((levels,)),
        ]
        + [pltpu.VMEM((share, cols, depth, part), f32)] * (levels * streams),
        compiler_params=pltpu.CompilerParams(
            collective_id=0, has_side_effects=True, vmem_limit_bytes=48 * 1024 * 1024
        ),
    )(rhs_low, rhs_top, inv_low, inv_top, blocks, table)
    return (sol_low[None, :, None], sol_top[None])


def solution(mesh):
    in_specs = (
        P("rep", None, "row", "col", None),
        P("row", "col", None),
        P("rep", None, "row", "col", None),
        P("row", "col", None),
        P("rep", "row", "col", None, None, None, None),
        P("rep", "row", "col", None, None, None),
    )
    out_specs = (P("rep", None, "row", "col", None), P("row", "col", None))
    body = functools.partial(per_device, mesh.shape["row"], mesh.shape["col"], mesh.shape["rep"])
    return jax.shard_map(body, mesh=mesh, in_specs=in_specs, out_specs=out_specs, check_vma=False)
```

```python
import functools
import jax
import jax.numpy as jnp
from jax import lax
from jax.experimental import pallas as pl
from jax.experimental.pallas import tpu as pltpu
from jax.sharding import PartitionSpec as P

MESH = pl.DeviceIdType.MESH
STREAMS = 4
GROUPS = 2
CROSSED = 3


def split(value):
    high = value.astype(jnp.bfloat16)
    low = (value - high.astype(jnp.float32)).astype(jnp.bfloat16)
    return high, low


def dot3(value, right_high, right_low):
    high, low = split(value)
    count = value.shape[0]
    turned = (((1,), (1,)), ((), ()))
    both = jnp.concatenate([high, low], axis=0)
    wide = lax.dot_general(both, right_high, turned, preferred_element_type=jnp.float32)
    rest = lax.dot_general(high, right_low, turned, preferred_element_type=jnp.float32)
    return wide[:count] + (wide[count:] + rest)


def kernel(
    rows, cols, reps, levels, slots, streams, groups,
    rhs_low, rhs_top, inv_low_hbm, inv_top_hbm, blocks_hbm, table_hbm, out_low, out_top,
    table, blocks, inverse, rhs, turned0, right0, partial, give, taken, taken_top, solved, handed, inv_high, inv_rest,
    tile_high, tile_rest,
    table_sem, load_sem, inv_sem, rhs_sem, right_send, right_recv, inv_send, inv_recv, give_send, give_recv,
    top_send, top_recv, col_send, col_recv, hand_send, hand_recv, *columns,
):
    row = lax.axis_index("row")
    q = lax.axis_index("col")
    rep = lax.axis_index("rep")
    share = rows // cols
    group = share // groups
    a = row // cols
    b = row % cols
    home = a // group
    place = a % group
    part = rhs_top.shape[0]
    depth = partial.shape[2]

    def turn(value, by, size):
        return lax.rem(value + by, size)

    def node_row(which, position, line):
        return (which * group + position) * cols + line

    loads = [
        pltpu.make_async_copy(blocks_hbm.at[l], blocks.at[l], load_sem.at[l]) for l in range(levels)
    ]
    inv_loads = [
        pltpu.make_async_copy(inv_low_hbm.at[t] if t < levels else inv_top_hbm, inverse.at[t, q], inv_sem.at[t])
        for t in range(levels + 1)
    ]
    rhs_loads = [
        pltpu.make_async_copy(rhs_low.at[t] if t < levels else rhs_top, rhs.at[t], rhs_sem.at[min(t, 1)])
        for t in range(levels + 1)
    ]
    table_load = pltpu.make_async_copy(table_hbm, table, table_sem)
    for load in [rhs_loads[0], inv_loads[0], inv_loads[1], loads[0]] + rhs_loads[1:] + inv_loads[2:] + loads[1:]:
        load.start()
    table_load.start()

    barrier = pltpu.get_barrier_semaphore()
    peers = set()
    for da in range(group):
        for dx in range(cols):
            for dy in range(cols):
                peers.add((0, da, dx, dy, 0))
    for e in range(groups):
        for dy in range(cols):
            peers.add((e, 0, 0, dy, 0))
    for dy in range(cols):
        for dc in range(reps):
            peers.add((0, 0, 0, dy, dc))
    peers.discard((0, 0, 0, 0, 0))
    for e, da, dx, dy, dc in sorted(peers):
        pl.semaphore_signal(
            barrier, inc=1, device_id_type=MESH,
            device_id={
                "row": node_row(turn(home, e, groups), turn(place, da, group), turn(b, dx, cols)),
                "col": turn(q, dy, cols), "rep": turn(rep, dc, reps),
            },
        )

    def send(src, dst, send_sem, recv_sem, device):
        return pltpu.make_async_remote_copy(
            src_ref=src, dst_ref=dst, send_sem=send_sem, recv_sem=recv_sem,
            device_id=device, device_id_type=MESH,
        )

    def finish(ref, sem):
        pltpu.make_async_copy(ref, ref, sem).wait()

    with jax.named_scope("turn_rhs"):
        finish(rhs.at[0], rhs_sem.at[0])
        first = rhs[0].T
        for s in range(streams):
            turned0[s] = first[s * depth:(s + 1) * depth]
    with jax.named_scope("barrier"):
        pl.semaphore_wait(barrier, len(peers))

    for s in range(streams):
        for d in range(1, cols):
            send(
                turned0.at[s], right0.at[s, cols - d], right_send, right_recv.at[s], {"col": turn(q, d, cols)}
            ).start()

    def give_inverse(t):
        finish(inverse.at[t, q], inv_sem.at[t])
        for d in range(1, cols):
            send(
                inverse.at[t, q], inverse.at[t, q], inv_send, inv_recv.at[t - 1, cols - d], {"col": turn(q, d, cols)}
            ).start()

    def take_inverse(t):
        for d in range(1, cols):
            finish(inverse.at[t, turn(q, d, cols)], inv_recv.at[t - 1, d])
        for h in range(cols):
            high, low = split(inverse[t, h])
            inv_high[t, h * part:(h + 1) * part] = high
            inv_rest[t, h * part:(h + 1) * part] = low

    def take_rhs(t):
        flipped = rhs[t].T
        if t == levels:
            flipped = jnp.where(rep == 0, flipped, 0.0)
        spaced = jnp.concatenate([jnp.where(q == j, flipped, 0.0) for j in range(cols)], axis=1)
        for s in range(streams):
            partial[t, s] = spaced[s * depth:(s + 1) * depth]

    def split_blocks(l):
        finish(blocks.at[l], load_sem.at[l])
        for k in range(slots):
            high, low = split(blocks[l, k])
            tile_high[k] = high
            tile_rest[k] = low

    def crossed(t, s):
        return t > 0 and s < CROSSED

    def offers(t, s):
        for e in reversed(range(groups)):
            for d in reversed(range(cols)):
                if (t == 0 and d) or not (e or d or crossed(t, s)):
                    continue
                h, back = turn(q, d, cols), (groups - e) % groups
                if crossed(t, s):
                    line, col, slot = h, b, lax.rem(q - b + cols, cols)
                else:
                    line, col, slot = b, h, (cols - d) % cols
                copy = send(
                    give.at[t, s, h], taken.at[t, s, back, slot], give_send.at[e, d], give_recv.at[t, s, back],
                    {"row": node_row(turn(home, e, groups), place, line), "col": col},
                )
                if e or d:
                    copy.start()
                else:
                    pl.when(q != b)(copy.start)

                    @pl.when(q == b)
                    def _():
                        pltpu.make_async_copy(give.at[t, s, q], taken.at[t, s, 0, 0], give_recv.at[t, s, 0]).start()

    def contribute(t, s):
        product = dot3(partial[t, s], inv_high[t], inv_rest[t])
        for h in range(cols):
            give[t, s, h] = product[:, h * part:(h + 1) * part]

    def gather(t, s, e):
        if t == 0:
            low, high = 0, 1 if e else 0
        else:
            low, high = 0 if e or crossed(t, s) else 1, cols
        total = None if e or crossed(t, s) else give[t, s, q]
        if high > low:
            with jax.named_scope("gather%d%d%d" % (t, s, e)):
                finish(taken.at[t, s, e, low:high], give_recv.at[t, s, e])
        for d in range(low, high):
            total = taken[t, s, e, d] if total is None else total + taken[t, s, e, d]
        return total

    def spread(l, s, e):
        which = turn(home, e, groups)
        line, col, piece = (q, q, b) if crossed(l, s) else (b, b, q)
        for da in reversed(range(group)):
            for dx in reversed(range(cols)):
                src = solved.at[l * streams + s, e]
                dst = columns[l * streams + s].at[which * group + place, piece]
                device = {"row": node_row(home, turn(place, da, group), turn(b, dx, cols)), "col": col}
                copy = functools.partial(send, src, dst, col_send.at[da, dx], col_recv.at[l, s], device)
                local = functools.partial(pltpu.make_async_copy, src, dst, col_recv.at[l, s])
                if da or dx:
                    copy().start()
                elif crossed(l, s):
                    local().start()
                else:
                    pl.when(q != b)(lambda: copy().start())
                    pl.when(q == b)(lambda: local().start())

    def hand_over(l, s):
        src = solved.at[l * streams + s, 0]
        copy = send(
            src, handed.at[l, s], hand_send, hand_recv.at[l], {"row": node_row(home, place, q), "col": b}
        )
        pl.when(q != b)(copy.start)

        @pl.when(q == b)
        def _():
            pltpu.make_async_copy(src, handed.at[l, s], hand_recv.at[l]).start()

    finish(inverse.at[0, q], inv_sem.at[0])
    high0, low0 = split(inverse[0, q])
    give_inverse(1)
    for s in range(streams):
        with jax.named_scope("rhs_wait%d" % s):
            finish(right0.at[s, 1:cols], right_recv.at[s])
        right0[s, 0] = turned0[s]
        residue = jnp.concatenate([right0[s, turn(cols - q, j, cols)] for j in range(cols)], axis=1)
        give[0, s, q] = dot3(residue, high0, low0)
        offers(0, s)
    table_load.wait()
    split_blocks(0)

    kept = []
    for l in range(levels):
        pieces = []
        for s in range(streams):
            for e in range(groups):
                total = gather(l, s, e)
                if e == 0 and not crossed(l, s):
                    pieces.append(total)
                solved[l * streams + s, e] = total
                spread(l, s, e)
        for s in range(streams):
            if crossed(l, s):
                hand_over(l, s)
        if l == 0:
            with jax.named_scope("take_rhs"):
                finish(rhs.at[1:], rhs_sem.at[1])
                for t in range(1, levels + 1):
                    take_rhs(t)
        if l == 0 or CROSSED == 0:
            out_low[l] = jnp.concatenate(pieces, axis=0).T
        else:
            kept.append((l, pieces))
        later = []

        def add(t, s, products):
            total = partial[t, s]
            for k in range(slots):
                total = total - jnp.where(table[l, 0, k] == t, products[k], 0.0)
            partial[t, s] = total

        for s in range(streams):
            with jax.named_scope("arrive%d%d" % (l, s)):
                finish(columns[l * streams + s], col_recv.at[l, s])
            with jax.named_scope("multiply%d%d" % (l, s)):
                products = []
                for k in range(slots):
                    found = columns[l * streams + s][table[l, 1, k]]
                    picked = jnp.concatenate([found[j] for j in range(cols)], axis=1)
                    products.append(dot3(picked, tile_high[k], tile_rest[k]))
                later.append((s, products))
                add(l + 1, s, products)
            if s == 0:
                with jax.named_scope("inverse%d" % l):
                    take_inverse(l + 1)
            with jax.named_scope("contribute%d%d" % (l, s)):
                contribute(l + 1, s)
            if l + 1 < levels:
                offers(l + 1, s)
            else:
                for d in reversed(range(cols)):
                    for r in reversed(range(reps)):
                        if d or r:
                            slot = (cols - d) % cols * reps + (reps - r) % reps - 1
                            send(
                                give.at[levels, s, turn(q, d, cols)], taken_top.at[s, slot], top_send,
                                top_recv.at[s], {"col": turn(q, d, cols), "rep": turn(rep, r, reps)},
                            ).start()
        for s, products in later:
            for t in range(l + 2, levels + 1):
                add(t, s, products)
        if l + 1 < levels:
            give_inverse(l + 2)
            split_blocks(l + 1)

    for l, pieces in kept:
        finish(handed.at[l, :CROSSED], hand_recv.at[l])
        out_low[l] = jnp.concatenate([handed[l, s] for s in range(CROSSED)] + pieces, axis=0).T
    pieces = []
    for s in range(streams):
        with jax.named_scope("top%d" % s):
            finish(taken_top.at[s], top_recv.at[s])
        total = give[levels, s, q]
        for slot in range(cols * reps - 1):
            total = total + taken_top[s, slot]
        pieces.append(total)
    with jax.named_scope("finish"):
        out_top[...] = jnp.concatenate(pieces, axis=0).T

        finish(right0.at[:, 1:cols], right_send)
        finish(inverse.at[1:, 1:cols], inv_send)
        finish(taken_top, top_send)
        for e in range(groups):
            for d in range(cols):
                if e or d:
                    finish(give.at[0 if d == 0 else 1:levels, :, 0], give_send.at[e, d])
        for da in range(group):
            for dx in range(cols):
                if da or dx:
                    finish(solved, col_send.at[da, dx])

        @pl.when(q != b)
        def _():
            plain = levels * streams - (levels - 1) * CROSSED
            finish(solved.at[:plain], col_send.at[0, 0])
            if CROSSED:
                finish(give.at[1:levels, :CROSSED, 0], give_send.at[0, 0])
                finish(handed.at[1:levels, :CROSSED], hand_send)


def per_device(rows, cols, reps, rhs_low, rhs_top, inv_low, inv_top, blocks, slot_map):
    rhs_low, rhs_top = rhs_low[0, :, 0], rhs_top[0]
    inv_low, inv_top = inv_low[0, :, 0], inv_top[0]
    blocks, table = blocks[0, 0, 0], jnp.swapaxes(slot_map[0, 0, 0], 1, 2)
    levels, slots, size = blocks.shape[:3]
    rhs_low, rhs_top, inv_low, inv_top, blocks, table = [
        pltpu.with_memory_space_constraint(x, pltpu.HBM) for x in (rhs_low, rhs_top, inv_low, inv_top, blocks, table)
    ]
    part, width = rhs_top.shape
    share = rows // cols
    streams, groups = STREAMS, GROUPS
    group = share // groups
    depth = width // streams
    vmem = pl.BlockSpec(memory_space=pltpu.VMEM)
    hbm = pl.BlockSpec(memory_space=pltpu.HBM)
    dma = pltpu.SemaphoreType.DMA
    f32, bf16 = jnp.float32, jnp.bfloat16
    sol_low, sol_top = pl.pallas_call(
        functools.partial(kernel, rows, cols, reps, levels, slots, streams, groups),
        out_shape=(
            jax.ShapeDtypeStruct((levels, part, width), f32),
            jax.ShapeDtypeStruct((part, width), f32),
        ),
        in_specs=[hbm, hbm, hbm, hbm, hbm, hbm],
        out_specs=(vmem, vmem),
        scratch_shapes=[
            pltpu.SMEM(table.shape, jnp.int32),
            pltpu.VMEM((levels, slots, size, size), f32),
            pltpu.VMEM((levels + 1, cols, part, size), f32),
            pltpu.VMEM((levels + 1, part, width), f32),
            pltpu.VMEM((streams, depth, part), f32),
            pltpu.VMEM((streams, cols, depth, part), f32),
            pltpu.VMEM((levels + 1, streams, depth, size), f32),
            pltpu.VMEM((levels + 1, streams, cols, depth, part), f32),
            pltpu.VMEM((levels, streams, groups, cols, depth, part), f32),
            pltpu.VMEM((streams, cols * reps - 1, depth, part), f32),
            pltpu.VMEM((levels * streams, groups, depth, part), f32),
            pltpu.VMEM((levels, streams, depth, part), f32),
            pltpu.VMEM((levels + 1, size, size), bf16),
            pltpu.VMEM((levels + 1, size, size), bf16),
            pltpu.VMEM((slots, size, size), bf16),
            pltpu.VMEM((slots, size, size), bf16),
            dma(()),
            dma((levels,)),
            dma((levels + 1,)),
            dma((2,)),
            dma(()),
            dma((streams,)),
            dma(()),
            dma((levels, cols)),
            dma((groups, cols)),
            dma((levels, streams, groups)),
            dma(()),
            dma((streams,)),
            dma((group, cols)),
            dma((levels, streams)),
            dma(()),
            dma((levels,)),
        ]
        + [pltpu.VMEM((share, cols, depth, part), f32)] * (levels * streams),
        compiler_params=pltpu.CompilerParams(
            collective_id=0, has_side_effects=True, vmem_limit_bytes=48 * 1024 * 1024
        ),
    )(rhs_low, rhs_top, inv_low, inv_top, blocks, table)
    return (sol_low[None, :, None], sol_top[None])


def solution(mesh):
    in_specs = (
        P("rep", None, "row", "col", None),
        P("row", "col", None),
        P("rep", None, "row", "col", None),
        P("row", "col", None),
        P("rep", "row", "col", None, None, None, None),
        P("rep", "row", "col", None, None, None),
    )
    out_specs = (P("rep", None, "row", "col", None), P("row", "col", None))
    body = functools.partial(per_device, mesh.shape["row"], mesh.shape["col"], mesh.shape["rep"])
    return jax.shard_map(body, mesh=mesh, in_specs=in_specs, out_specs=out_specs, check_vma=False)
```

```python
import functools
import jax
import jax.numpy as jnp
from jax import lax
from jax.experimental import pallas as pl
from jax.experimental.pallas import tpu as pltpu
from jax.sharding import PartitionSpec as P

MESH = pl.DeviceIdType.MESH
STREAMS = 4
GROUPS = 2
CROSSED = 4
CROSSED_FIRST = 0


def split(value):
    high = value.astype(jnp.bfloat16)
    low = (value - high.astype(jnp.float32)).astype(jnp.bfloat16)
    return high, low


def dot3(value, right_high, right_low):
    high, low = split(value)
    count = value.shape[0]
    turned = (((1,), (1,)), ((), ()))
    both = jnp.concatenate([high, low], axis=0)
    wide = lax.dot_general(both, right_high, turned, preferred_element_type=jnp.float32)
    rest = lax.dot_general(high, right_low, turned, preferred_element_type=jnp.float32)
    return wide[:count] + (wide[count:] + rest)


def kernel(
    rows, cols, reps, levels, slots, streams, groups,
    rhs_low, rhs_top, inv_low_hbm, inv_top_hbm, blocks_hbm, table_hbm, out_low, out_top,
    table, blocks, inverse, rhs, turned0, right0, partial, give, taken, taken_top, solved, handed, inv_high, inv_rest,
    tile_high, tile_rest,
    table_sem, load_sem, inv_sem, rhs_sem, right_send, right_recv, inv_send, inv_recv, give_send, give_recv,
    top_send, top_recv, col_send, col_recv, hand_send, hand_recv, *columns,
):
    row = lax.axis_index("row")
    q = lax.axis_index("col")
    rep = lax.axis_index("rep")
    share = rows // cols
    group = share // groups
    a = row // cols
    b = row % cols
    home = a // group
    place = a % group
    part = rhs_top.shape[0]
    depth = partial.shape[2]

    def turn(value, by, size):
        return lax.rem(value + by, size)

    def node_row(which, position, line):
        return (which * group + position) * cols + line

    loads = [
        pltpu.make_async_copy(blocks_hbm.at[l], blocks.at[l], load_sem.at[l]) for l in range(levels)
    ]
    inv_loads = [
        pltpu.make_async_copy(inv_low_hbm.at[t] if t < levels else inv_top_hbm, inverse.at[t, q], inv_sem.at[t])
        for t in range(levels + 1)
    ]
    rhs_loads = [
        pltpu.make_async_copy(rhs_low.at[t] if t < levels else rhs_top, rhs.at[t], rhs_sem.at[min(t, 1)])
        for t in range(levels + 1)
    ]
    table_load = pltpu.make_async_copy(table_hbm, table, table_sem)
    rhs_loads[0].start()

    barrier = pltpu.get_barrier_semaphore()
    peers = set()
    for da in range(group):
        for dx in range(cols):
            peers.add((0, da, dx, 0, 0))
    for e in range(groups):
        peers.add((e, 0, 0, 0, 0))
    for dy in range(cols):
        peers.add((0, 0, 0, dy, 0))
    for dc in range(reps):
        peers.add((0, 0, 0, 0, dc))
    peers.discard((0, 0, 0, 0, 0))
    for e, da, dx, dy, dc in sorted(peers):
        pl.semaphore_signal(
            barrier, inc=1, device_id_type=MESH,
            device_id={
                "row": node_row(turn(home, e, groups), turn(place, da, group), turn(b, dx, cols)),
                "col": turn(q, dy, cols), "rep": turn(rep, dc, reps),
            },
        )

    for load in [inv_loads[0], inv_loads[1], loads[0]] + rhs_loads[1:] + inv_loads[2:] + loads[1:]:
        load.start()
    table_load.start()

    def send(src, dst, send_sem, recv_sem, device):
        return pltpu.make_async_remote_copy(
            src_ref=src, dst_ref=dst, send_sem=send_sem, recv_sem=recv_sem,
            device_id=device, device_id_type=MESH,
        )

    def finish(ref, sem):
        pltpu.make_async_copy(ref, ref, sem).wait()

    with jax.named_scope("turn_rhs"):
        finish(rhs.at[0], rhs_sem.at[0])
        first = rhs[0].T
        for s in range(streams):
            turned0[s] = first[s * depth:(s + 1) * depth]
    with jax.named_scope("barrier"):
        pl.semaphore_wait(barrier, len(peers))

    for s in range(streams):
        for d in range(1, cols):
            send(
                turned0.at[s], right0.at[s, cols - d], right_send, right_recv.at[s], {"col": turn(q, d, cols)}
            ).start()

    def give_inverse(t, i, count):
        if i == 0:
            finish(inverse.at[t, q], inv_sem.at[t])
        cut = pl.ds(i * (part // count), part // count)
        for d in range(1, cols):
            send(
                inverse.at[t, q, cut], inverse.at[t, q, cut], inv_send, inv_recv.at[t - 1, cols - d],
                {"col": turn(q, d, cols)},
            ).start()

    def take_inverse(t):
        for d in range(1, cols):
            finish(inverse.at[t, turn(q, d, cols)], inv_recv.at[t - 1, d])
        for h in range(cols):
            high, low = split(inverse[t, h])
            inv_high[t, h * part:(h + 1) * part] = high
            inv_rest[t, h * part:(h + 1) * part] = low

    def take_rhs(t):
        flipped = rhs[t].T
        if t == levels:
            flipped = jnp.where(rep == 0, flipped, 0.0)
        spaced = jnp.concatenate([jnp.where(q == j, flipped, 0.0) for j in range(cols)], axis=1)
        for s in range(streams):
            partial[t, s] = spaced[s * depth:(s + 1) * depth]

    def split_blocks(l):
        finish(blocks.at[l], load_sem.at[l])
        for k in range(slots):
            high, low = split(blocks[l, k])
            tile_high[k] = high
            tile_rest[k] = low

    def crossed(t, s):
        return s < (CROSSED if t else CROSSED_FIRST)

    def offers(t, s):
        for e in reversed(range(groups)):
            for d in reversed(range(cols)):
                if (t == 0 and d) or not (e or d or crossed(t, s)):
                    continue
                h, back = turn(q, d, cols), (groups - e) % groups
                if crossed(t, s):
                    line, col, slot = h, b, lax.rem(q - b + cols, cols) if t else 0
                else:
                    line, col, slot = b, h, (cols - d) % cols
                copy = send(
                    give.at[t, s, h], taken.at[t, s, back, slot], give_send.at[e, d], give_recv.at[t, s, back],
                    {"row": node_row(turn(home, e, groups), place, line), "col": col},
                )
                if e or d:
                    copy.start()
                else:
                    pl.when(q != b)(copy.start)

                    @pl.when(q == b)
                    def _():
                        pltpu.make_async_copy(give.at[t, s, q], taken.at[t, s, 0, 0], give_recv.at[t, s, 0]).start()

    def contribute(t, s):
        product = dot3(partial[t, s], inv_high[t], inv_rest[t])
        for h in range(cols):
            give[t, s, h] = product[:, h * part:(h + 1) * part]

    def gather(t, s, e):
        mine = not (e or crossed(t, s))
        low, high = (0, 0 if mine else 1) if t == 0 else (1 if mine else 0, cols)
        total = give[t, s, q] if mine else None
        if high > low:
            with jax.named_scope("gather%d%d%d" % (t, s, e)):
                finish(taken.at[t, s, e, low:high], give_recv.at[t, s, e])
        for d in range(low, high):
            total = taken[t, s, e, d] if total is None else total + taken[t, s, e, d]
        return total

    def spread(l, s, e):
        which = turn(home, e, groups)
        line, col, piece = (q, q, b) if crossed(l, s) else (b, b, q)
        for da in reversed(range(group)):
            for dx in reversed(range(cols)):
                src = solved.at[l * streams + s, e]
                dst = columns[l * streams + s].at[which * group + place, piece]
                device = {"row": node_row(home, turn(place, da, group), turn(b, dx, cols)), "col": col}
                copy = functools.partial(send, src, dst, col_send.at[da, dx], col_recv.at[l, s], device)
                local = functools.partial(pltpu.make_async_copy, src, dst, col_recv.at[l, s])
                if da or dx:
                    copy().start()
                elif crossed(l, s):
                    local().start()
                else:
                    pl.when(q != b)(lambda: copy().start())
                    pl.when(q == b)(lambda: local().start())

    def hand_over(l, s):
        src = solved.at[l * streams + s, 0]
        copy = send(
            src, handed.at[l, s], hand_send, hand_recv.at[l], {"row": node_row(home, place, q), "col": b}
        )
        pl.when(q != b)(copy.start)

        @pl.when(q == b)
        def _():
            pltpu.make_async_copy(src, handed.at[l, s], hand_recv.at[l]).start()

    finish(inverse.at[0, q], inv_sem.at[0])
    high0, low0 = split(inverse[0, q])
    give_inverse(1, 0, 1)
    for s in range(streams):
        with jax.named_scope("rhs_wait%d" % s):
            finish(right0.at[s, 1:cols], right_recv.at[s])
        right0[s, 0] = turned0[s]
        residue = jnp.concatenate([right0[s, turn(cols - q, j, cols)] for j in range(cols)], axis=1)
        give[0, s, q] = dot3(residue, high0, low0)
        offers(0, s)
    table_load.wait()
    split_blocks(0)

    kept = []
    for l in range(levels):
        pieces = []
        for s in range(streams):
            for e in range(groups):
                total = gather(l, s, e)
                if e == 0 and l == 0:
                    pieces.append(give[0, s, q])
                elif e == 0 and not crossed(l, s):
                    pieces.append(total)
                solved[l * streams + s, e] = total
                spread(l, s, e)
        for s in range(streams):
            if l and crossed(l, s):
                hand_over(l, s)
        if l == 0:
            with jax.named_scope("take_rhs"):
                finish(rhs.at[1:], rhs_sem.at[1])
                for t in range(1, levels + 1):
                    take_rhs(t)
        if l == 0 or CROSSED == 0:
            out_low[l] = jnp.concatenate(pieces, axis=0).T
        else:
            kept.append((l, pieces))
        later = []

        def add(t, s, products):
            total = partial[t, s]
            for k in range(slots):
                total = total - jnp.where(table[l, 0, k] == t, products[k], 0.0)
            partial[t, s] = total

        for s in range(streams):
            with jax.named_scope("arrive%d%d" % (l, s)):
                finish(columns[l * streams + s], col_recv.at[l, s])
            with jax.named_scope("multiply%d%d" % (l, s)):
                products = []
                for k in range(slots):
                    found = columns[l * streams + s][table[l, 1, k]]
                    picked = jnp.concatenate([found[j] for j in range(cols)], axis=1)
                    products.append(dot3(picked, tile_high[k], tile_rest[k]))
                later.append((s, products))
                add(l + 1, s, products)
            if s == 0:
                with jax.named_scope("inverse%d" % l):
                    take_inverse(l + 1)
            with jax.named_scope("contribute%d%d" % (l, s)):
                contribute(l + 1, s)
            if l + 1 < levels:
                offers(l + 1, s)
                give_inverse(l + 2, s, streams)
            else:
                for d in reversed(range(cols)):
                    for r in reversed(range(reps)):
                        if d or r:
                            slot = (cols - d) % cols * reps + (reps - r) % reps - 1
                            send(
                                give.at[levels, s, turn(q, d, cols)], taken_top.at[s, slot], top_send,
                                top_recv.at[s], {"col": turn(q, d, cols), "rep": turn(rep, r, reps)},
                            ).start()
        for s, products in later:
            for t in range(l + 2, levels + 1):
                add(t, s, products)
        if l + 1 < levels:
            split_blocks(l + 1)

    for l, pieces in kept:
        finish(handed.at[l, :CROSSED], hand_recv.at[l])
        out_low[l] = jnp.concatenate([handed[l, s] for s in range(CROSSED)] + pieces, axis=0).T
    pieces = []
    for s in range(streams):
        with jax.named_scope("top%d" % s):
            finish(taken_top.at[s], top_recv.at[s])
        total = give[levels, s, q]
        for slot in range(cols * reps - 1):
            total = total + taken_top[s, slot]
        pieces.append(total)
    with jax.named_scope("finish"):
        out_top[...] = jnp.concatenate(pieces, axis=0).T

        finish(right0.at[:, 1:cols], right_send)
        finish(inverse.at[1:, 1:cols], inv_send)
        finish(taken_top, top_send)
        for e in range(groups):
            for d in range(cols):
                if e or d:
                    finish(give.at[0 if d == 0 else 1:levels, :, 0], give_send.at[e, d])
        for da in range(group):
            for dx in range(cols):
                if da or dx:
                    finish(solved, col_send.at[da, dx])

        @pl.when(q != b)
        def _():
            plain = levels * streams - (levels - 1) * CROSSED - CROSSED_FIRST
            finish(solved.at[:plain], col_send.at[0, 0])
            if CROSSED:
                finish(handed.at[1:levels, :CROSSED], hand_send)
            crossings = (levels - 1) * CROSSED + CROSSED_FIRST
            if crossings:
                finish(solved.at[:crossings, 0], give_send.at[0, 0])


def per_device(rows, cols, reps, rhs_low, rhs_top, inv_low, inv_top, blocks, slot_map):
    rhs_low, rhs_top = rhs_low[0, :, 0], rhs_top[0]
    inv_low, inv_top = inv_low[0, :, 0], inv_top[0]
    blocks, table = blocks[0, 0, 0], jnp.swapaxes(slot_map[0, 0, 0], 1, 2)
    levels, slots, size = blocks.shape[:3]
    rhs_low, rhs_top, inv_low, inv_top, blocks, table = [
        pltpu.with_memory_space_constraint(x, pltpu.HBM) for x in (rhs_low, rhs_top, inv_low, inv_top, blocks, table)
    ]
    part, width = rhs_top.shape
    share = rows // cols
    streams, groups = STREAMS, GROUPS
    group = share // groups
    depth = width // streams
    vmem = pl.BlockSpec(memory_space=pltpu.VMEM)
    hbm = pl.BlockSpec(memory_space=pltpu.HBM)
    dma = pltpu.SemaphoreType.DMA
    f32, bf16 = jnp.float32, jnp.bfloat16
    sol_low, sol_top = pl.pallas_call(
        functools.partial(kernel, rows, cols, reps, levels, slots, streams, groups),
        out_shape=(
            jax.ShapeDtypeStruct((levels, part, width), f32),
            jax.ShapeDtypeStruct((part, width), f32),
        ),
        in_specs=[hbm, hbm, hbm, hbm, hbm, hbm],
        out_specs=(vmem, vmem),
        scratch_shapes=[
            pltpu.SMEM(table.shape, jnp.int32),
            pltpu.VMEM((levels, slots, size, size), f32),
            pltpu.VMEM((levels + 1, cols, part, size), f32),
            pltpu.VMEM((levels + 1, part, width), f32),
            pltpu.VMEM((streams, depth, part), f32),
            pltpu.VMEM((streams, cols, depth, part), f32),
            pltpu.VMEM((levels + 1, streams, depth, size), f32),
            pltpu.VMEM((levels + 1, streams, cols, depth, part), f32),
            pltpu.VMEM((levels, streams, groups, cols, depth, part), f32),
            pltpu.VMEM((streams, cols * reps - 1, depth, part), f32),
            pltpu.VMEM((levels * streams, groups, depth, part), f32),
            pltpu.VMEM((levels, streams, depth, part), f32),
            pltpu.VMEM((levels + 1, size, size), bf16),
            pltpu.VMEM((levels + 1, size, size), bf16),
            pltpu.VMEM((slots, size, size), bf16),
            pltpu.VMEM((slots, size, size), bf16),
            dma(()),
            dma((levels,)),
            dma((levels + 1,)),
            dma((2,)),
            dma(()),
            dma((streams,)),
            dma(()),
            dma((levels, cols)),
            dma((groups, cols)),
            dma((levels, streams, groups)),
            dma(()),
            dma((streams,)),
            dma((group, cols)),
            dma((levels, streams)),
            dma(()),
            dma((levels,)),
        ]
        + [pltpu.VMEM((share, cols, depth, part), f32)] * (levels * streams),
        compiler_params=pltpu.CompilerParams(
            collective_id=0, has_side_effects=True, vmem_limit_bytes=48 * 1024 * 1024
        ),
    )(rhs_low, rhs_top, inv_low, inv_top, blocks, table)
    return (sol_low[None, :, None], sol_top[None])


def solution(mesh):
    in_specs = (
        P("rep", None, "row", "col", None),
        P("row", "col", None),
        P("rep", None, "row", "col", None),
        P("row", "col", None),
        P("rep", "row", "col", None, None, None, None),
        P("rep", "row", "col", None, None, None),
    )
    out_specs = (P("rep", None, "row", "col", None), P("row", "col", None))
    body = functools.partial(per_device, mesh.shape["row"], mesh.shape["col"], mesh.shape["rep"])
    return jax.shard_map(body, mesh=mesh, in_specs=in_specs, out_specs=out_specs, check_vma=False)
```

```python
import functools
import jax
import jax.numpy as jnp
from jax import lax
from jax.experimental import pallas as pl
from jax.experimental.pallas import tpu as pltpu
from jax.sharding import PartitionSpec as P

MESH = pl.DeviceIdType.MESH
STREAMS = 4
GROUPS = 2
CROSSED = 4
CROSSED_FIRST = 0


def split(value):
    high = value.astype(jnp.bfloat16)
    low = (value - high.astype(jnp.float32)).astype(jnp.bfloat16)
    return high, low


def dot3(value, right_high, right_low):
    high, low = split(value)
    count = value.shape[0]
    turned = (((1,), (1,)), ((), ()))
    both = jnp.concatenate([high, low], axis=0)
    wide = lax.dot_general(both, right_high, turned, preferred_element_type=jnp.float32)
    rest = lax.dot_general(high, right_low, turned, preferred_element_type=jnp.float32)
    return wide[:count] + (wide[count:] + rest)


def kernel(
    rows, cols, reps, levels, slots, streams, groups,
    rhs_low, rhs_top, inv_low_hbm, inv_top_hbm, blocks_hbm, table_hbm, out_low, out_top,
    table, blocks, inverse, rhs, turned0, right0, partial, give, taken, taken_top, solved, handed, inv_high, inv_rest,
    tile_high, tile_rest,
    table_sem, load_sem, inv_sem, rhs_sem, right_send, right_recv, inv_send, inv_recv, give_send, give_recv,
    top_send, top_recv, col_send, col_recv, hand_send, hand_recv, *columns,
):
    row = lax.axis_index("row")
    q = lax.axis_index("col")
    rep = lax.axis_index("rep")
    share = rows // cols
    group = share // groups
    a = row // cols
    b = row % cols
    home = a // group
    place = a % group
    part = rhs_top.shape[0]
    depth = partial.shape[2]

    def turn(value, by, size):
        return lax.rem(value + by, size)

    def node_row(which, position, line):
        return (which * group + position) * cols + line

    loads = [
        pltpu.make_async_copy(blocks_hbm.at[l], blocks.at[l], load_sem.at[l]) for l in range(levels)
    ]
    inv_loads = [
        pltpu.make_async_copy(inv_low_hbm.at[t] if t < levels else inv_top_hbm, inverse.at[t, q], inv_sem.at[t])
        for t in range(levels + 1)
    ]
    rhs_loads = [
        pltpu.make_async_copy(rhs_low.at[t] if t < levels else rhs_top, rhs.at[t], rhs_sem.at[min(t, 1)])
        for t in range(levels + 1)
    ]
    table_load = pltpu.make_async_copy(table_hbm, table, table_sem)
    rhs_loads[0].start()

    barrier = pltpu.get_barrier_semaphore()
    peers = set()
    for da in range(group):
        for dx in range(cols):
            peers.add((0, da, dx, 0, 0))
    for e in range(groups):
        peers.add((e, 0, 0, 0, 0))
    for dy in range(cols):
        peers.add((0, 0, 0, dy, 0))
    for dc in range(reps):
        peers.add((0, 0, 0, 0, dc))
    peers.discard((0, 0, 0, 0, 0))
    for e, da, dx, dy, dc in sorted(peers):
        pl.semaphore_signal(
            barrier, inc=1, device_id_type=MESH,
            device_id={
                "row": node_row(turn(home, e, groups), turn(place, da, group), turn(b, dx, cols)),
                "col": turn(q, dy, cols), "rep": turn(rep, dc, reps),
            },
        )

    for load in [inv_loads[0], inv_loads[1], loads[0]] + rhs_loads[1:] + inv_loads[2:] + loads[1:]:
        load.start()
    table_load.start()

    def send(src, dst, send_sem, recv_sem, device):
        return pltpu.make_async_remote_copy(
            src_ref=src, dst_ref=dst, send_sem=send_sem, recv_sem=recv_sem,
            device_id=device, device_id_type=MESH,
        )

    def finish(ref, sem):
        pltpu.make_async_copy(ref, ref, sem).wait()

    with jax.named_scope("turn_rhs"):
        finish(rhs.at[0], rhs_sem.at[0])
        first = rhs[0].T
        for s in range(streams):
            turned0[s] = first[s * depth:(s + 1) * depth]
    with jax.named_scope("barrier"):
        pl.semaphore_wait(barrier, len(peers))

    for s in range(streams):
        for d in range(1, cols):
            send(
                turned0.at[s], right0.at[s, cols - d], right_send, right_recv.at[s], {"col": turn(q, d, cols)}
            ).start()

    def give_inverse(t, i, count):
        if i == 0:
            finish(inverse.at[t, q], inv_sem.at[t])
        cut = pl.ds(i * (part // count), part // count)
        for d in range(1, cols):
            send(
                inverse.at[t, q, cut], inverse.at[t, q, cut], inv_send, inv_recv.at[t - 1, cols - d],
                {"col": turn(q, d, cols)},
            ).start()

    def take_inverse(t):
        for d in range(1, cols):
            finish(inverse.at[t, turn(q, d, cols)], inv_recv.at[t - 1, d])
        for h in range(cols):
            high, low = split(inverse[t, h])
            inv_high[t, h * part:(h + 1) * part] = high
            inv_rest[t, h * part:(h + 1) * part] = low

    def take_rhs(t):
        flipped = rhs[t].T
        if t == levels:
            flipped = jnp.where(rep == 0, flipped, 0.0)
        spaced = jnp.concatenate([jnp.where(q == j, flipped, 0.0) for j in range(cols)], axis=1)
        for s in range(streams):
            partial[t, s] = spaced[s * depth:(s + 1) * depth]

    def split_blocks(l):
        finish(blocks.at[l], load_sem.at[l])
        for k in range(slots):
            high, low = split(blocks[l, k])
            tile_high[k] = high
            tile_rest[k] = low

    def crossed(t, s):
        return s < (CROSSED if t else CROSSED_FIRST)

    def offers(t, s):
        for e in reversed(range(groups)):
            for d in reversed(range(cols)):
                if (t == 0 and d) or not (e or d or crossed(t, s)):
                    continue
                h, back = turn(q, d, cols), (groups - e) % groups
                if crossed(t, s):
                    line, col, slot = h, b, lax.rem(q - b + cols, cols) if t else 0
                else:
                    line, col, slot = b, h, (cols - d) % cols
                copy = send(
                    give.at[t, s, h], taken.at[t, s, back, slot], give_send.at[e, d], give_recv.at[t, s, back],
                    {"row": node_row(turn(home, e, groups), place, line), "col": col},
                )
                if e or d:
                    copy.start()
                else:
                    pl.when(q != b)(copy.start)

                    @pl.when(q == b)
                    def _():
                        pltpu.make_async_copy(give.at[t, s, q], taken.at[t, s, 0, 0], give_recv.at[t, s, 0]).start()

    def contribute(t, s):
        product = dot3(partial[t, s], inv_high[t], inv_rest[t])
        for h in range(cols):
            give[t, s, h] = product[:, h * part:(h + 1) * part]

    def gather(t, s, e):
        mine = not (e or crossed(t, s))
        low, high = (0, 0 if mine else 1) if t == 0 else (1 if mine else 0, cols)
        total = give[t, s, q] if mine else None
        if high > low:
            with jax.named_scope("gather%d%d%d" % (t, s, e)):
                finish(taken.at[t, s, e, low:high], give_recv.at[t, s, e])
        for d in range(low, high):
            total = taken[t, s, e, d] if total is None else total + taken[t, s, e, d]
        return total

    def spread(l, s, e):
        which = turn(home, e, groups)
        line, col, piece = (q, q, b) if crossed(l, s) else (b, b, q)
        for da in reversed(range(group)):
            for dx in reversed(range(cols)):
                src = solved.at[l * streams + s, e]
                dst = columns[l * streams + s].at[which * group + place, piece]
                device = {"row": node_row(home, turn(place, da, group), turn(b, dx, cols)), "col": col}
                copy = functools.partial(send, src, dst, col_send.at[da, dx], col_recv.at[l, s], device)
                local = functools.partial(pltpu.make_async_copy, src, dst, col_recv.at[l, s])
                if da or dx:
                    copy().start()
                elif crossed(l, s):
                    local().start()
                else:
                    pl.when(q != b)(lambda: copy().start())
                    pl.when(q == b)(lambda: local().start())

    def hand_over(l, s):
        src = solved.at[l * streams + s, 0]
        copy = send(
            src, handed.at[l, s], hand_send, hand_recv.at[l], {"row": node_row(home, place, q), "col": b}
        )
        pl.when(q != b)(copy.start)

        @pl.when(q == b)
        def _():
            pltpu.make_async_copy(src, handed.at[l, s], hand_recv.at[l]).start()

    finish(inverse.at[0, q], inv_sem.at[0])
    high0, low0 = split(inverse[0, q])
    give_inverse(1, 0, 1)
    for s in range(streams):
        with jax.named_scope("rhs_wait%d" % s):
            finish(right0.at[s, 1:cols], right_recv.at[s])
        right0[s, 0] = turned0[s]
        residue = jnp.concatenate([right0[s, turn(cols - q, j, cols)] for j in range(cols)], axis=1)
        give[0, s, q] = dot3(residue, high0, low0)
        offers(0, s)
    table_load.wait()
    split_blocks(0)

    kept = []
    for l in range(levels):
        pieces = []
        for s in range(streams):
            for e in range(groups):
                total = gather(l, s, e)
                if e == 0 and l == 0:
                    pieces.append(give[0, s, q])
                elif e == 0 and not crossed(l, s):
                    pieces.append(total)
                solved[l * streams + s, e] = total
                spread(l, s, e)
        for s in range(streams):
            if l and crossed(l, s):
                hand_over(l, s)
        if l == 0:
            with jax.named_scope("take_rhs"):
                finish(rhs.at[1:], rhs_sem.at[1])
                for t in range(1, levels + 1):
                    take_rhs(t)
        if l == 0 or CROSSED == 0:
            out_low[l] = jnp.concatenate(pieces, axis=0).T
        else:
            kept.append((l, pieces))
        later = []

        def add(t, s, products):
            total = partial[t, s]
            for k in range(slots):
                total = total - jnp.where(table[l, 0, k] == t, products[k], 0.0)
            partial[t, s] = total

        for s in range(streams):
            with jax.named_scope("arrive%d%d" % (l, s)):
                finish(columns[l * streams + s], col_recv.at[l, s])
            with jax.named_scope("multiply%d%d" % (l, s)):
                products = []
                for k in range(slots):
                    found = columns[l * streams + s][table[l, 1, k]]
                    picked = jnp.concatenate([found[j] for j in range(cols)], axis=1)
                    products.append(dot3(picked, tile_high[k], tile_rest[k]))
                later.append((s, products))
                add(l + 1, s, products)
            if s == 0:
                with jax.named_scope("inverse%d" % l):
                    take_inverse(l + 1)
            with jax.named_scope("contribute%d%d" % (l, s)):
                contribute(l + 1, s)
            if l + 1 < levels:
                offers(l + 1, s)
                if s >= streams // 2:
                    give_inverse(l + 2, s - streams // 2, streams // 2)
            else:
                for d in reversed(range(cols)):
                    for r in reversed(range(reps)):
                        if d or r:
                            slot = (cols - d) % cols * reps + (reps - r) % reps - 1
                            send(
                                give.at[levels, s, turn(q, d, cols)], taken_top.at[s, slot], top_send,
                                top_recv.at[s], {"col": turn(q, d, cols), "rep": turn(rep, r, reps)},
                            ).start()
        for s, products in later:
            for t in range(l + 2, levels + 1):
                add(t, s, products)
        if l + 1 < levels:
            split_blocks(l + 1)

    for l, pieces in kept:
        finish(handed.at[l, :CROSSED], hand_recv.at[l])
        out_low[l] = jnp.concatenate([handed[l, s] for s in range(CROSSED)] + pieces, axis=0).T
    pieces = []
    for s in range(streams):
        with jax.named_scope("top%d" % s):
            finish(taken_top.at[s], top_recv.at[s])
        total = give[levels, s, q]
        for slot in range(cols * reps - 1):
            total = total + taken_top[s, slot]
        pieces.append(total)
    with jax.named_scope("finish"):
        out_top[...] = jnp.concatenate(pieces, axis=0).T

        finish(right0.at[:, 1:cols], right_send)
        finish(inverse.at[1:, 1:cols], inv_send)
        finish(taken_top, top_send)
        for e in range(groups):
            for d in range(cols):
                if e or d:
                    finish(give.at[0 if d == 0 else 1:levels, :, 0], give_send.at[e, d])
        for da in range(group):
            for dx in range(cols):
                if da or dx:
                    finish(solved, col_send.at[da, dx])

        @pl.when(q != b)
        def _():
            plain = levels * streams - (levels - 1) * CROSSED - CROSSED_FIRST
            finish(solved.at[:plain], col_send.at[0, 0])
            if CROSSED:
                finish(handed.at[1:levels, :CROSSED], hand_send)
            crossings = (levels - 1) * CROSSED + CROSSED_FIRST
            if crossings:
                finish(solved.at[:crossings, 0], give_send.at[0, 0])


def per_device(rows, cols, reps, rhs_low, rhs_top, inv_low, inv_top, blocks, slot_map):
    rhs_low, rhs_top = rhs_low[0, :, 0], rhs_top[0]
    inv_low, inv_top = inv_low[0, :, 0], inv_top[0]
    blocks, table = blocks[0, 0, 0], jnp.swapaxes(slot_map[0, 0, 0], 1, 2)
    levels, slots, size = blocks.shape[:3]
    rhs_low, rhs_top, inv_low, inv_top, blocks, table = [
        pltpu.with_memory_space_constraint(x, pltpu.HBM) for x in (rhs_low, rhs_top, inv_low, inv_top, blocks, table)
    ]
    part, width = rhs_top.shape
    share = rows // cols
    streams, groups = STREAMS, GROUPS
    group = share // groups
    depth = width // streams
    vmem = pl.BlockSpec(memory_space=pltpu.VMEM)
    hbm = pl.BlockSpec(memory_space=pltpu.HBM)
    dma = pltpu.SemaphoreType.DMA
    f32, bf16 = jnp.float32, jnp.bfloat16
    sol_low, sol_top = pl.pallas_call(
        functools.partial(kernel, rows, cols, reps, levels, slots, streams, groups),
        out_shape=(
            jax.ShapeDtypeStruct((levels, part, width), f32),
            jax.ShapeDtypeStruct((part, width), f32),
        ),
        in_specs=[hbm, hbm, hbm, hbm, hbm, hbm],
        out_specs=(vmem, vmem),
        scratch_shapes=[
            pltpu.SMEM(table.shape, jnp.int32),
            pltpu.VMEM((levels, slots, size, size), f32),
            pltpu.VMEM((levels + 1, cols, part, size), f32),
            pltpu.VMEM((levels + 1, part, width), f32),
            pltpu.VMEM((streams, depth, part), f32),
            pltpu.VMEM((streams, cols, depth, part), f32),
            pltpu.VMEM((levels + 1, streams, depth, size), f32),
            pltpu.VMEM((levels + 1, streams, cols, depth, part), f32),
            pltpu.VMEM((levels, streams, groups, cols, depth, part), f32),
            pltpu.VMEM((streams, cols * reps - 1, depth, part), f32),
            pltpu.VMEM((levels * streams, groups, depth, part), f32),
            pltpu.VMEM((levels, streams, depth, part), f32),
            pltpu.VMEM((levels + 1, size, size), bf16),
            pltpu.VMEM((levels + 1, size, size), bf16),
            pltpu.VMEM((slots, size, size), bf16),
            pltpu.VMEM((slots, size, size), bf16),
            dma(()),
            dma((levels,)),
            dma((levels + 1,)),
            dma((2,)),
            dma(()),
            dma((streams,)),
            dma(()),
            dma((levels, cols)),
            dma((groups, cols)),
            dma((levels, streams, groups)),
            dma(()),
            dma((streams,)),
            dma((group, cols)),
            dma((levels, streams)),
            dma(()),
            dma((levels,)),
        ]
        + [pltpu.VMEM((share, cols, depth, part), f32)] * (levels * streams),
        compiler_params=pltpu.CompilerParams(
            collective_id=0, has_side_effects=True, vmem_limit_bytes=48 * 1024 * 1024
        ),
    )(rhs_low, rhs_top, inv_low, inv_top, blocks, table)
    return (sol_low[None, :, None], sol_top[None])


def solution(mesh):
    in_specs = (
        P("rep", None, "row", "col", None),
        P("row", "col", None),
        P("rep", None, "row", "col", None),
        P("row", "col", None),
        P("rep", "row", "col", None, None, None, None),
        P("rep", "row", "col", None, None, None),
    )
    out_specs = (P("rep", None, "row", "col", None), P("row", "col", None))
    body = functools.partial(per_device, mesh.shape["row"], mesh.shape["col"], mesh.shape["rep"])
    return jax.shard_map(body, mesh=mesh, in_specs=in_specs, out_specs=out_specs, check_vma=False)
```

```python
import functools
import jax
import jax.numpy as jnp
from jax import lax
from jax.experimental import pallas as pl
from jax.experimental.pallas import tpu as pltpu
from jax.sharding import PartitionSpec as P

MESH = pl.DeviceIdType.MESH
STREAMS = 4
GROUPS = 2
CROSSED = 4
CROSSED_FIRST = 0


def split(value):
    high = value.astype(jnp.bfloat16)
    low = (value - high.astype(jnp.float32)).astype(jnp.bfloat16)
    return high, low


def dot3(value, right_high, right_low):
    high, low = split(value)
    count = value.shape[0]
    turned = (((1,), (1,)), ((), ()))
    both = jnp.concatenate([high, low], axis=0)
    wide = lax.dot_general(both, right_high, turned, preferred_element_type=jnp.float32)
    rest = lax.dot_general(high, right_low, turned, preferred_element_type=jnp.float32)
    return wide[:count] + (wide[count:] + rest)


def kernel(
    rows, cols, reps, levels, slots, streams, groups,
    rhs_low, rhs_top, inv_low_hbm, inv_top_hbm, blocks_hbm, table_hbm, out_low, out_top,
    table, blocks, inverse, rhs, turned0, right0, partial, give, taken, taken_top, solved, handed, inv_high, inv_rest,
    tile_high, tile_rest,
    table_sem, load_sem, inv_sem, rhs_sem, right_send, right_recv, inv_send, inv_recv, give_send, give_recv,
    top_send, top_recv, col_send, col_recv, hand_send, hand_recv, *columns,
):
    row = lax.axis_index("row")
    q = lax.axis_index("col")
    rep = lax.axis_index("rep")
    share = rows // cols
    group = share // groups
    a = row // cols
    b = row % cols
    home = a // group
    place = a % group
    part = rhs_top.shape[0]
    depth = partial.shape[2]

    def turn(value, by, size):
        return lax.rem(value + by, size)

    def node_row(which, position, line):
        return (which * group + position) * cols + line

    loads = [
        pltpu.make_async_copy(blocks_hbm.at[l], blocks.at[l], load_sem.at[l]) for l in range(levels)
    ]
    inv_loads = [
        pltpu.make_async_copy(inv_low_hbm.at[t] if t < levels else inv_top_hbm, inverse.at[t, q], inv_sem.at[min(t, 1)])
        for t in range(levels + 1)
    ]
    rhs_loads = [
        pltpu.make_async_copy(rhs_low.at[t] if t < levels else rhs_top, rhs.at[t], rhs_sem.at[min(t, 1)])
        for t in range(levels + 1)
    ]
    table_load = pltpu.make_async_copy(table_hbm, table, table_sem)
    rhs_loads[0].start()

    barrier = pltpu.get_barrier_semaphore()
    peers = set()
    for da in range(group):
        for dx in range(cols):
            peers.add((0, da, dx, 0, 0))
    for e in range(groups):
        peers.add((e, 0, 0, 0, 0))
    for dy in range(cols):
        peers.add((0, 0, 0, dy, 0))
    for dc in range(reps):
        peers.add((0, 0, 0, 0, dc))
    peers.discard((0, 0, 0, 0, 0))
    for e, da, dx, dy, dc in sorted(peers):
        pl.semaphore_signal(
            barrier, inc=1, device_id_type=MESH,
            device_id={
                "row": node_row(turn(home, e, groups), turn(place, da, group), turn(b, dx, cols)),
                "col": turn(q, dy, cols), "rep": turn(rep, dc, reps),
            },
        )

    for load in [inv_loads[0], inv_loads[1], loads[0]] + rhs_loads[1:] + inv_loads[2:] + loads[1:]:
        load.start()
    table_load.start()

    def send(src, dst, send_sem, recv_sem, device):
        return pltpu.make_async_remote_copy(
            src_ref=src, dst_ref=dst, send_sem=send_sem, recv_sem=recv_sem,
            device_id=device, device_id_type=MESH,
        )

    def finish(ref, sem):
        pltpu.make_async_copy(ref, ref, sem).wait()

    with jax.named_scope("turn_rhs"):
        finish(rhs.at[0], rhs_sem.at[0])
        first = rhs[0].T
        for s in range(streams):
            turned0[s] = first[s * depth:(s + 1) * depth]
    with jax.named_scope("barrier"):
        pl.semaphore_wait(barrier, len(peers))

    for s in range(streams):
        for d in range(1, cols):
            send(
                turned0.at[s], right0.at[s, cols - d], right_send, right_recv.at[s], {"col": turn(q, d, cols)}
            ).start()

    def give_inverse(t, i, count):
        if t == 1 and i == 0:
            finish(inverse.at[1:, q], inv_sem.at[1])
        cut = pl.ds(i * (part // count), part // count)
        for d in range(1, cols):
            send(
                inverse.at[t, q, cut], inverse.at[t, q, cut], inv_send, inv_recv.at[t - 1, cols - d - 1],
                {"col": turn(q, d, cols)},
            ).start()

    def take_inverse(t):
        for d in range(1, cols):
            finish(inverse.at[t, turn(q, d, cols)], inv_recv.at[t - 1, d - 1])
        for h in range(cols):
            high, low = split(inverse[t, h])
            inv_high[t, h * part:(h + 1) * part] = high
            inv_rest[t, h * part:(h + 1) * part] = low

    def take_rhs(t):
        flipped = rhs[t].T
        if t == levels:
            flipped = jnp.where(rep == 0, flipped, 0.0)
        spaced = jnp.concatenate([jnp.where(q == j, flipped, 0.0) for j in range(cols)], axis=1)
        for s in range(streams):
            partial[t, s] = spaced[s * depth:(s + 1) * depth]

    def split_blocks(l):
        finish(blocks.at[l], load_sem.at[l])
        for k in range(slots):
            high, low = split(blocks[l, k])
            tile_high[k] = high
            tile_rest[k] = low

    def crossed(t, s):
        return s < (CROSSED if t else CROSSED_FIRST)

    def offers(t, s):
        for e in reversed(range(groups)):
            for d in reversed(range(cols)):
                if (t == 0 and d) or not (e or d or crossed(t, s)):
                    continue
                h, back = turn(q, d, cols), (groups - e) % groups
                if crossed(t, s):
                    line, col, slot = h, b, lax.rem(q - b + cols, cols) if t else 0
                else:
                    line, col, slot = b, h, (cols - d) % cols
                copy = send(
                    give.at[t, s, h], taken.at[t, s, back, slot], give_send.at[e, d], give_recv.at[t, s, back],
                    {"row": node_row(turn(home, e, groups), place, line), "col": col},
                )
                if e or d:
                    copy.start()
                else:
                    pl.when(q != b)(copy.start)

                    @pl.when(q == b)
                    def _():
                        pltpu.make_async_copy(give.at[t, s, q], taken.at[t, s, 0, 0], give_recv.at[t, s, 0]).start()

    def contribute(t, s):
        product = dot3(partial[t, s], inv_high[t], inv_rest[t])
        for h in range(cols):
            give[t, s, h] = product[:, h * part:(h + 1) * part]

    def gather(t, s, e):
        mine = not (e or crossed(t, s))
        low, high = (0, 0 if mine else 1) if t == 0 else (1 if mine else 0, cols)
        total = give[t, s, q] if mine else None
        if high > low:
            with jax.named_scope("gather%d%d%d" % (t, s, e)):
                finish(taken.at[t, s, e, low:high], give_recv.at[t, s, e])
        for d in range(low, high):
            total = taken[t, s, e, d] if total is None else total + taken[t, s, e, d]
        return total

    def spread(l, s, e):
        which = turn(home, e, groups)
        line, col, piece = (q, q, b) if crossed(l, s) else (b, b, q)
        for da in reversed(range(group)):
            for dx in reversed(range(cols)):
                src = solved.at[l * streams + s, e]
                dst = columns[l * streams + s].at[which * group + place, piece]
                device = {"row": node_row(home, turn(place, da, group), turn(b, dx, cols)), "col": col}
                copy = functools.partial(send, src, dst, col_send.at[da, dx], col_recv.at[l, s], device)
                local = functools.partial(pltpu.make_async_copy, src, dst, col_recv.at[l, s])
                if da or dx:
                    copy().start()
                elif crossed(l, s):
                    local().start()
                else:
                    pl.when(q != b)(lambda: copy().start())
                    pl.when(q == b)(lambda: local().start())

    def hand_over(l, s):
        src = solved.at[l * streams + s, 0]
        copy = send(
            src, handed.at[l, s], hand_send, hand_recv, {"row": node_row(home, place, q), "col": b}
        )
        pl.when(q != b)(copy.start)

        @pl.when(q == b)
        def _():
            pltpu.make_async_copy(src, handed.at[l, s], hand_recv).start()

    finish(inverse.at[0, q], inv_sem.at[0])
    high0, low0 = split(inverse[0, q])
    give_inverse(1, 0, 1)
    for s in range(streams):
        with jax.named_scope("rhs_wait%d" % s):
            finish(right0.at[s, 1:cols], right_recv.at[s])
        right0[s, 0] = turned0[s]
        residue = jnp.concatenate([right0[s, turn(cols - q, j, cols)] for j in range(cols)], axis=1)
        give[0, s, q] = dot3(residue, high0, low0)
        offers(0, s)
    table_load.wait()
    split_blocks(0)

    kept = []
    for l in range(levels):
        pieces = []
        for s in range(streams):
            for e in range(groups):
                total = gather(l, s, e)
                if e == 0 and l == 0:
                    pieces.append(give[0, s, q])
                elif e == 0 and not crossed(l, s):
                    pieces.append(total)
                solved[l * streams + s, e] = total
                spread(l, s, e)
        for s in range(streams):
            if l and crossed(l, s):
                hand_over(l, s)
        if l == 0:
            with jax.named_scope("take_rhs"):
                finish(rhs.at[1:], rhs_sem.at[1])
                for t in range(1, levels + 1):
                    take_rhs(t)
        if l == 0 or CROSSED == 0:
            out_low[l] = jnp.concatenate(pieces, axis=0).T
        else:
            kept.append((l, pieces))
        later = []

        def add(t, s, products):
            total = partial[t, s]
            for k in range(slots):
                total = total - jnp.where(table[l, 0, k] == t, products[k], 0.0)
            partial[t, s] = total

        for s in range(streams):
            with jax.named_scope("arrive%d%d" % (l, s)):
                finish(columns[l * streams + s], col_recv.at[l, s])
            with jax.named_scope("multiply%d%d" % (l, s)):
                products = []
                for k in range(slots):
                    found = columns[l * streams + s][table[l, 1, k]]
                    picked = jnp.concatenate([found[j] for j in range(cols)], axis=1)
                    products.append(dot3(picked, tile_high[k], tile_rest[k]))
                later.append((s, products))
                add(l + 1, s, products)
            if s == 0:
                with jax.named_scope("inverse%d" % l):
                    take_inverse(l + 1)
            with jax.named_scope("contribute%d%d" % (l, s)):
                contribute(l + 1, s)
            if l + 1 < levels:
                offers(l + 1, s)
                if s >= streams // 2:
                    give_inverse(l + 2, s - streams // 2, streams // 2)
            else:
                for d in reversed(range(cols)):
                    for r in reversed(range(reps)):
                        if d or r:
                            slot = (cols - d) % cols * reps + (reps - r) % reps - 1
                            send(
                                give.at[levels, s, turn(q, d, cols)], taken_top.at[s, slot], top_send,
                                top_recv.at[s], {"col": turn(q, d, cols), "rep": turn(rep, r, reps)},
                            ).start()
        for s, products in later:
            for t in range(l + 2, levels + 1):
                add(t, s, products)
        if l + 1 < levels:
            split_blocks(l + 1)

    if kept:
        finish(handed.at[1:levels, :CROSSED], hand_recv)
    for l, pieces in kept:
        out_low[l] = jnp.concatenate([handed[l, s] for s in range(CROSSED)] + pieces, axis=0).T
    pieces = []
    for s in range(streams):
        with jax.named_scope("top%d" % s):
            finish(taken_top.at[s], top_recv.at[s])
        total = give[levels, s, q]
        for slot in range(cols * reps - 1):
            total = total + taken_top[s, slot]
        pieces.append(total)
    with jax.named_scope("finish"):
        out_top[...] = jnp.concatenate(pieces, axis=0).T

        finish(right0.at[:, 1:cols], right_send)
        finish(inverse.at[1:, 1:cols], inv_send)
        finish(taken_top, top_send)
        for e in range(groups):
            for d in range(cols):
                if e or d:
                    finish(give.at[0 if d == 0 else 1:levels, :, 0], give_send.at[e, d])
        for da in range(group):
            for dx in range(cols):
                if da or dx:
                    finish(solved, col_send.at[da, dx])

        @pl.when(q != b)
        def _():
            plain = levels * streams - (levels - 1) * CROSSED - CROSSED_FIRST
            finish(solved.at[:plain], col_send.at[0, 0])
            if CROSSED:
                finish(handed.at[1:levels, :CROSSED], hand_send)
            crossings = (levels - 1) * CROSSED + CROSSED_FIRST
            if crossings:
                finish(solved.at[:crossings, 0], give_send.at[0, 0])


def per_device(rows, cols, reps, rhs_low, rhs_top, inv_low, inv_top, blocks, slot_map):
    rhs_low, rhs_top = rhs_low[0, :, 0], rhs_top[0]
    inv_low, inv_top = inv_low[0, :, 0], inv_top[0]
    blocks, table = blocks[0, 0, 0], jnp.swapaxes(slot_map[0, 0, 0], 1, 2)
    levels, slots, size = blocks.shape[:3]
    rhs_low, rhs_top, inv_low, inv_top, blocks, table = [
        pltpu.with_memory_space_constraint(x, pltpu.HBM) for x in (rhs_low, rhs_top, inv_low, inv_top, blocks, table)
    ]
    part, width = rhs_top.shape
    share = rows // cols
    streams, groups = STREAMS, GROUPS
    group = share // groups
    depth = width // streams
    vmem = pl.BlockSpec(memory_space=pltpu.VMEM)
    hbm = pl.BlockSpec(memory_space=pltpu.HBM)
    dma = pltpu.SemaphoreType.DMA
    f32, bf16 = jnp.float32, jnp.bfloat16
    sol_low, sol_top = pl.pallas_call(
        functools.partial(kernel, rows, cols, reps, levels, slots, streams, groups),
        out_shape=(
            jax.ShapeDtypeStruct((levels, part, width), f32),
            jax.ShapeDtypeStruct((part, width), f32),
        ),
        in_specs=[hbm, hbm, hbm, hbm, hbm, hbm],
        out_specs=(vmem, vmem),
        scratch_shapes=[
            pltpu.SMEM(table.shape, jnp.int32),
            pltpu.VMEM((levels, slots, size, size), f32),
            pltpu.VMEM((levels + 1, cols, part, size), f32),
            pltpu.VMEM((levels + 1, part, width), f32),
            pltpu.VMEM((streams, depth, part), f32),
            pltpu.VMEM((streams, cols, depth, part), f32),
            pltpu.VMEM((levels + 1, streams, depth, size), f32),
            pltpu.VMEM((levels + 1, streams, cols, depth, part), f32),
            pltpu.VMEM((levels, streams, groups, cols, depth, part), f32),
            pltpu.VMEM((streams, cols * reps - 1, depth, part), f32),
            pltpu.VMEM((levels * streams, groups, depth, part), f32),
            pltpu.VMEM((levels, streams, depth, part), f32),
            pltpu.VMEM((levels + 1, size, size), bf16),
            pltpu.VMEM((levels + 1, size, size), bf16),
            pltpu.VMEM((slots, size, size), bf16),
            pltpu.VMEM((slots, size, size), bf16),
            dma(()),
            dma((levels,)),
            dma((2,)),
            dma((2,)),
            dma(()),
            dma((streams,)),
            dma(()),
            dma((levels, cols - 1)),
            dma((groups, cols)),
            dma((levels, streams, groups)),
            dma(()),
            dma((streams,)),
            dma((group, cols)),
            dma((levels, streams)),
            dma(()),
            dma(()),
        ]
        + [pltpu.VMEM((share, cols, depth, part), f32)] * (levels * streams),
        compiler_params=pltpu.CompilerParams(
            collective_id=0, has_side_effects=True, vmem_limit_bytes=48 * 1024 * 1024
        ),
    )(rhs_low, rhs_top, inv_low, inv_top, blocks, table)
    return (sol_low[None, :, None], sol_top[None])


def solution(mesh):
    in_specs = (
        P("rep", None, "row", "col", None),
        P("row", "col", None),
        P("rep", None, "row", "col", None),
        P("row", "col", None),
        P("rep", "row", "col", None, None, None, None),
        P("rep", "row", "col", None, None, None),
    )
    out_specs = (P("rep", None, "row", "col", None), P("row", "col", None))
    body = functools.partial(per_device, mesh.shape["row"], mesh.shape["col"], mesh.shape["rep"])
    return jax.shard_map(body, mesh=mesh, in_specs=in_specs, out_specs=out_specs, check_vma=False)
```

```python
import functools
import jax
import jax.numpy as jnp
from jax import lax
from jax.experimental import pallas as pl
from jax.experimental.pallas import tpu as pltpu
from jax.sharding import PartitionSpec as P

MESH = pl.DeviceIdType.MESH
STREAMS = 4
GROUPS = 2
CROSSED = 4
CROSSED_FIRST = 0


def split(value):
    high = value.astype(jnp.bfloat16)
    low = (value - high.astype(jnp.float32)).astype(jnp.bfloat16)
    return high, low


def dot3(value, right_high, right_low):
    high, low = split(value)
    count = value.shape[0]
    turned = (((1,), (1,)), ((), ()))
    both = jnp.concatenate([high, low], axis=0)
    wide = lax.dot_general(both, right_high, turned, preferred_element_type=jnp.float32)
    rest = lax.dot_general(high, right_low, turned, preferred_element_type=jnp.float32)
    return wide[:count] + (wide[count:] + rest)


def kernel(
    rows, cols, reps, levels, slots, streams, groups,
    rhs_low, rhs_top, inv_low_hbm, inv_top_hbm, blocks_hbm, table_hbm, out_low, out_top,
    table, blocks, inverse, rhs, turned0, right0, partial, give, taken, taken_top, solved, handed, inv_high, inv_rest,
    tile_high, tile_rest,
    table_sem, load_sem, inv_sem, rhs_sem, right_send, right_recv, inv_send, inv_recv, give_send, give_recv,
    top_send, top_recv, col_send, col_recv, hand_send, hand_recv, *columns,
):
    row = lax.axis_index("row")
    q = lax.axis_index("col")
    rep = lax.axis_index("rep")
    share = rows // cols
    group = share // groups
    a = row // cols
    b = row % cols
    home = a // group
    place = a % group
    part = rhs_top.shape[0]
    depth = partial.shape[2]

    def turn(value, by, size):
        return lax.rem(value + by, size)

    def node_row(which, position, line):
        return (which * group + position) * cols + line

    loads = [
        pltpu.make_async_copy(blocks_hbm.at[l], blocks.at[l], load_sem.at[l]) for l in range(levels)
    ]
    inv_loads = [
        pltpu.make_async_copy(inv_low_hbm.at[t] if t < levels else inv_top_hbm, inverse.at[t, q], inv_sem.at[t])
        for t in range(levels + 1)
    ]
    rhs_loads = [
        pltpu.make_async_copy(rhs_low.at[t] if t < levels else rhs_top, rhs.at[t], rhs_sem.at[min(t, 1)])
        for t in range(levels + 1)
    ]
    table_load = pltpu.make_async_copy(table_hbm, table, table_sem)
    rhs_loads[0].start()

    barrier = pltpu.get_barrier_semaphore()
    peers = set()
    for da in range(group):
        for dx in range(cols):
            peers.add((0, da, dx, 0, 0))
    for e in range(groups):
        peers.add((e, 0, 0, 0, 0))
    for dy in range(cols):
        peers.add((0, 0, 0, dy, 0))
    for dc in range(reps):
        peers.add((0, 0, 0, 0, dc))
    peers.discard((0, 0, 0, 0, 0))
    for e, da, dx, dy, dc in sorted(peers):
        pl.semaphore_signal(
            barrier, inc=1, device_id_type=MESH,
            device_id={
                "row": node_row(turn(home, e, groups), turn(place, da, group), turn(b, dx, cols)),
                "col": turn(q, dy, cols), "rep": turn(rep, dc, reps),
            },
        )

    for load in [inv_loads[0], inv_loads[1], loads[0]] + rhs_loads[1:] + inv_loads[2:] + loads[1:]:
        load.start()
    table_load.start()

    def send(src, dst, send_sem, recv_sem, device):
        return pltpu.make_async_remote_copy(
            src_ref=src, dst_ref=dst, send_sem=send_sem, recv_sem=recv_sem,
            device_id=device, device_id_type=MESH,
        )

    def finish(ref, sem):
        pltpu.make_async_copy(ref, ref, sem).wait()

    with jax.named_scope("turn_rhs"):
        finish(rhs.at[0], rhs_sem.at[0])
        first = rhs[0].T
        for s in range(streams):
            turned0[s] = first[s * depth:(s + 1) * depth]
    with jax.named_scope("barrier"):
        pl.semaphore_wait(barrier, len(peers))

    for s in range(streams):
        for d in range(1, cols):
            send(
                turned0.at[s], right0.at[s, cols - d], right_send, right_recv.at[s], {"col": turn(q, d, cols)}
            ).start()

    def give_inverse(t, i, count):
        if i == 0:
            finish(inverse.at[t, q], inv_sem.at[t])
        cut = pl.ds(i * (part // count), part // count)
        for d in range(1, cols):
            send(
                inverse.at[t, q, cut], inverse.at[t, q, cut], inv_send, inv_recv.at[t - 1, cols - d],
                {"col": turn(q, d, cols)},
            ).start()

    def take_inverse(t):
        for d in range(1, cols):
            finish(inverse.at[t, turn(q, d, cols)], inv_recv.at[t - 1, d])
        for h in range(cols):
            high, low = split(inverse[t, h])
            inv_high[t, h * part:(h + 1) * part] = high
            inv_rest[t, h * part:(h + 1) * part] = low

    def take_rhs(t):
        flipped = rhs[t].T
        if t == levels:
            flipped = jnp.where(rep == 0, flipped, 0.0)
        spaced = jnp.concatenate([jnp.where(q == j, flipped, 0.0) for j in range(cols)], axis=1)
        for s in range(streams):
            partial[t, s] = spaced[s * depth:(s + 1) * depth]

    def split_blocks(l):
        finish(blocks.at[l], load_sem.at[l])
        for k in range(slots):
            high, low = split(blocks[l, k])
            tile_high[k] = high
            tile_rest[k] = low

    def crossed(t, s):
        return s < (CROSSED if t else CROSSED_FIRST)

    def offers(t, s):
        for e in reversed(range(groups)):
            for d in reversed(range(cols)):
                if (t == 0 and d) or not (e or d or crossed(t, s)):
                    continue
                h, back = turn(q, d, cols), (groups - e) % groups
                if crossed(t, s):
                    line, col, slot = h, b, lax.rem(q - b + cols, cols) if t else 0
                else:
                    line, col, slot = b, h, (cols - d) % cols
                copy = send(
                    give.at[t, s, h], taken.at[t, s, back, slot], give_send.at[e, d], give_recv.at[t, s, back],
                    {"row": node_row(turn(home, e, groups), place, line), "col": col},
                )
                if e or d:
                    copy.start()
                else:
                    pl.when(q != b)(copy.start)

                    @pl.when(q == b)
                    def _():
                        pltpu.make_async_copy(give.at[t, s, q], taken.at[t, s, 0, 0], give_recv.at[t, s, 0]).start()

    def contribute(t, s):
        product = dot3(partial[t, s], inv_high[t], inv_rest[t])
        for h in range(cols):
            give[t, s, h] = product[:, h * part:(h + 1) * part]

    def gather(t, s, e):
        mine = not (e or crossed(t, s))
        low, high = (0, 0 if mine else 1) if t == 0 else (1 if mine else 0, cols)
        total = give[t, s, q] if mine else None
        if high > low:
            with jax.named_scope("gather%d%d%d" % (t, s, e)):
                finish(taken.at[t, s, e, low:high], give_recv.at[t, s, e])
        for d in range(low, high):
            total = taken[t, s, e, d] if total is None else total + taken[t, s, e, d]
        return total

    def spread(l, s, e):
        which = turn(home, e, groups)
        line, col, piece = (q, q, b) if crossed(l, s) else (b, b, q)
        for da in reversed(range(group)):
            for dx in reversed(range(cols)):
                src = solved.at[l * streams + s, e]
                dst = columns[l * streams + s].at[which * group + place, piece]
                device = {"row": node_row(home, turn(place, da, group), turn(b, dx, cols)), "col": col}
                copy = functools.partial(send, src, dst, col_send.at[da, dx], col_recv.at[l, s], device)
                local = functools.partial(pltpu.make_async_copy, src, dst, col_recv.at[l, s])
                if da or dx:
                    copy().start()
                elif crossed(l, s):
                    local().start()
                else:
                    pl.when(q != b)(lambda: copy().start())
                    pl.when(q == b)(lambda: local().start())

    def hand_over(l, s):
        src = solved.at[l * streams + s, 0]
        copy = send(
            src, handed.at[l, s], hand_send, hand_recv.at[l], {"row": node_row(home, place, q), "col": b}
        )
        pl.when(q != b)(copy.start)

        @pl.when(q == b)
        def _():
            pltpu.make_async_copy(src, handed.at[l, s], hand_recv.at[l]).start()

    finish(inverse.at[0, q], inv_sem.at[0])
    high0, low0 = split(inverse[0, q])
    give_inverse(1, 0, 1)
    for s in range(streams):
        with jax.named_scope("rhs_wait%d" % s):
            finish(right0.at[s, 1:cols], right_recv.at[s])
        right0[s, 0] = turned0[s]
        residue = jnp.concatenate([right0[s, turn(cols - q, j, cols)] for j in range(cols)], axis=1)
        give[0, s, q] = dot3(residue, high0, low0)
        offers(0, s)
    table_load.wait()
    split_blocks(0)

    kept = []
    for l in range(levels):
        pieces = []
        for s in range(streams):
            for e in range(groups):
                total = gather(l, s, e)
                if e == 0 and l == 0:
                    pieces.append(give[0, s, q])
                elif e == 0 and not crossed(l, s):
                    pieces.append(total)
                solved[l * streams + s, e] = total
                spread(l, s, e)
        for s in range(streams):
            if l and crossed(l, s):
                hand_over(l, s)
        if l == 0:
            with jax.named_scope("take_rhs"):
                finish(rhs.at[1:], rhs_sem.at[1])
                for t in range(1, levels + 1):
                    take_rhs(t)
        if l == 0 or CROSSED == 0:
            out_low[l] = jnp.concatenate(pieces, axis=0).T
        else:
            kept.append((l, pieces))
        later = []

        def add(t, s, products):
            total = partial[t, s]
            for k in range(slots):
                total = total - jnp.where(table[l, 0, k] == t, products[k], 0.0)
            partial[t, s] = total

        for s in range(streams):
            with jax.named_scope("arrive%d%d" % (l, s)):
                finish(columns[l * streams + s], col_recv.at[l, s])
            with jax.named_scope("multiply%d%d" % (l, s)):
                products = []
                for k in range(slots):
                    found = columns[l * streams + s][table[l, 1, k]]
                    picked = jnp.concatenate([found[j] for j in range(cols)], axis=1)
                    products.append(dot3(picked, tile_high[k], tile_rest[k]))
                later.append((s, products))
                add(l + 1, s, products)
            if s == 0:
                with jax.named_scope("inverse%d" % l):
                    take_inverse(l + 1)
            with jax.named_scope("contribute%d%d" % (l, s)):
                contribute(l + 1, s)
            if l + 1 < levels:
                offers(l + 1, s)
                if 1 <= s <= streams // 2:
                    give_inverse(l + 2, s - 1, streams // 2)
            else:
                for d in reversed(range(cols)):
                    for r in reversed(range(reps)):
                        if d or r:
                            slot = (cols - d) % cols * reps + (reps - r) % reps - 1
                            send(
                                give.at[levels, s, turn(q, d, cols)], taken_top.at[s, slot], top_send,
                                top_recv.at[s], {"col": turn(q, d, cols), "rep": turn(rep, r, reps)},
                            ).start()
        for s, products in later:
            for t in range(l + 2, levels + 1):
                add(t, s, products)
        if l + 1 < levels:
            split_blocks(l + 1)

    for l, pieces in kept:
        finish(handed.at[l, :CROSSED], hand_recv.at[l])
        out_low[l] = jnp.concatenate([handed[l, s] for s in range(CROSSED)] + pieces, axis=0).T
    pieces = []
    for s in range(streams):
        with jax.named_scope("top%d" % s):
            finish(taken_top.at[s], top_recv.at[s])
        total = give[levels, s, q]
        for slot in range(cols * reps - 1):
            total = total + taken_top[s, slot]
        pieces.append(total)
    with jax.named_scope("finish"):
        out_top[...] = jnp.concatenate(pieces, axis=0).T

        finish(right0.at[:, 1:cols], right_send)
        finish(inverse.at[1:, 1:cols], inv_send)
        finish(taken_top, top_send)
        for e in range(groups):
            for d in range(cols):
                if e or d:
                    finish(give.at[0 if d == 0 else 1:levels, :, 0], give_send.at[e, d])
        for da in range(group):
            for dx in range(cols):
                if da or dx:
                    finish(solved, col_send.at[da, dx])

        @pl.when(q != b)
        def _():
            plain = levels * streams - (levels - 1) * CROSSED - CROSSED_FIRST
            finish(solved.at[:plain], col_send.at[0, 0])
            if CROSSED:
                finish(handed.at[1:levels, :CROSSED], hand_send)
            crossings = (levels - 1) * CROSSED + CROSSED_FIRST
            if crossings:
                finish(solved.at[:crossings, 0], give_send.at[0, 0])


def per_device(rows, cols, reps, rhs_low, rhs_top, inv_low, inv_top, blocks, slot_map):
    rhs_low, rhs_top = rhs_low[0, :, 0], rhs_top[0]
    inv_low, inv_top = inv_low[0, :, 0], inv_top[0]
    blocks, table = blocks[0, 0, 0], jnp.swapaxes(slot_map[0, 0, 0], 1, 2)
    levels, slots, size = blocks.shape[:3]
    rhs_low, rhs_top, inv_low, inv_top, blocks, table = [
        pltpu.with_memory_space_constraint(x, pltpu.HBM) for x in (rhs_low, rhs_top, inv_low, inv_top, blocks, table)
    ]
    part, width = rhs_top.shape
    share = rows // cols
    streams, groups = STREAMS, GROUPS
    group = share // groups
    depth = width // streams
    vmem = pl.BlockSpec(memory_space=pltpu.VMEM)
    hbm = pl.BlockSpec(memory_space=pltpu.HBM)
    dma = pltpu.SemaphoreType.DMA
    f32, bf16 = jnp.float32, jnp.bfloat16
    sol_low, sol_top = pl.pallas_call(
        functools.partial(kernel, rows, cols, reps, levels, slots, streams, groups),
        out_shape=(
            jax.ShapeDtypeStruct((levels, part, width), f32),
            jax.ShapeDtypeStruct((part, width), f32),
        ),
        in_specs=[hbm, hbm, hbm, hbm, hbm, hbm],
        out_specs=(vmem, vmem),
        scratch_shapes=[
            pltpu.SMEM(table.shape, jnp.int32),
            pltpu.VMEM((levels, slots, size, size), f32),
            pltpu.VMEM((levels + 1, cols, part, size), f32),
            pltpu.VMEM((levels + 1, part, width), f32),
            pltpu.VMEM((streams, depth, part), f32),
            pltpu.VMEM((streams, cols, depth, part), f32),
            pltpu.VMEM((levels + 1, streams, depth, size), f32),
            pltpu.VMEM((levels + 1, streams, cols, depth, part), f32),
            pltpu.VMEM((levels, streams, groups, cols, depth, part), f32),
            pltpu.VMEM((streams, cols * reps - 1, depth, part), f32),
            pltpu.VMEM((levels * streams, groups, depth, part), f32),
            pltpu.VMEM((levels, streams, depth, part), f32),
            pltpu.VMEM((levels + 1, size, size), bf16),
            pltpu.VMEM((levels + 1, size, size), bf16),
            pltpu.VMEM((slots, size, size), bf16),
            pltpu.VMEM((slots, size, size), bf16),
            dma(()),
            dma((levels,)),
            dma((levels + 1,)),
            dma((2,)),
            dma(()),
            dma((streams,)),
            dma(()),
            dma((levels, cols)),
            dma((groups, cols)),
            dma((levels, streams, groups)),
            dma(()),
            dma((streams,)),
            dma((group, cols)),
            dma((levels, streams)),
            dma(()),
            dma((levels,)),
        ]
        + [pltpu.VMEM((share, cols, depth, part), f32)] * (levels * streams),
        compiler_params=pltpu.CompilerParams(
            collective_id=0, has_side_effects=True, vmem_limit_bytes=48 * 1024 * 1024
        ),
    )(rhs_low, rhs_top, inv_low, inv_top, blocks, table)
    return (sol_low[None, :, None], sol_top[None])


def solution(mesh):
    in_specs = (
        P("rep", None, "row", "col", None),
        P("row", "col", None),
        P("rep", None, "row", "col", None),
        P("row", "col", None),
        P("rep", "row", "col", None, None, None, None),
        P("rep", "row", "col", None, None, None),
    )
    out_specs = (P("rep", None, "row", "col", None), P("row", "col", None))
    body = functools.partial(per_device, mesh.shape["row"], mesh.shape["col"], mesh.shape["rep"])
    return jax.shard_map(body, mesh=mesh, in_specs=in_specs, out_specs=out_specs, check_vma=False)
```
